32 devices in a mesh: region: 4 (over y, core), shard: 8 (over z, x).
Axes of the slice: x: 2, y: 2, z: 4, core: 2. Of those that a mesh axis runs over, the one named last changes fastest.
Arguments:
- fields: bfloat16 [32, 16384], P('shard', 'region'), may hold values from -6 to 6
- near_coef: bfloat16 [128, 3, 128, 128], P(('region', 'shard')), may hold values from -0.25 to 0.25
- far_coef: bfloat16 [128, 2, 128, 128], P(('region', 'shard')), may hold values from -0.25 to 0.25
- inv_factor: bfloat16 [128, 128, 128], P(('region', 'shard')), as said below
- near_block: int32 [128, 3], P(('region', 'shard')), may hold values from 0 to 3, as said below
- far_region: int32 [128, 2], P(('region', 'shard')), may hold values from 0 to 3, all different within a row; in each aligned block of 4 rows (0 to 3, 4 to 7, ...) at most 2 rows name the same one
- far_block: int32 [128, 2], P(('region', 'shard')), may hold values from 0 to 3
Outputs:
- whitened: bfloat16 [32, 16384], P('shard', 'region')
The draws below stay inside these ranges and needn't reach their ends.
Inputs may be any that keep to these rules, and one draw needn't show every extreme that they name: inv_factor[g] is upper triangular with a positive diagonal. `near_block`: row g lists 3 different indices of its own group of 4 blocks, never g % 4 itself. `far_region`: each row names 2 different regions; within the rows of one group of 4 blocks no region is named more than 2 times.
All inputs are finite; a program needn't handle non-finite values.
Results may differ from the reference program's by a relative error of at most 0.0049.
Values may be sent and summed in bfloat16 or wider, within the bound.
A program may use at most 64 MiB of HBM per device.

```python
import math
import jax
import jax.numpy as jnp
import numpy as np
from jax import lax

BLOCK = 128
FAR = 2
BLK_DEV = 4
NEAR = 3
SAMPLES = 32
NBLK = 128
NLOC = 16384
CAP = 2
N_REGION = 4
N_SHARD = 8


def draw_inv_factor(key, part):
    key_off, key_diag = jax.random.split(key)
    row_index = jnp.arange(BLOCK)[:, None]
    col_index = jnp.arange(BLOCK)[None, :]
    upper = col_index > row_index
    on_diag = col_index == row_index
    spread = 0.7 / math.sqrt(BLOCK)
    offdiag = jax.random.normal(key_off, (NBLK, BLOCK, BLOCK), jnp.float32) * spread
    diagonal = jax.random.uniform(key_diag, (NBLK, 1, BLOCK), jnp.float32, 0.5, 2.0)
    matrix = jnp.where(upper, offdiag, 0.0) + jnp.where(on_diag, diagonal, 0.0)
    return matrix.astype(jnp.bfloat16)


def draw_near_block(key, part):
    row_keys = jax.random.split(key, NBLK)
    orders = jax.vmap(lambda one_key: jax.random.permutation(one_key, BLK_DEV - 1))(row_keys)[:, :NEAR]
    own_index = (jnp.arange(NBLK, dtype=jnp.int32) % BLK_DEV)[:, None]
    return (orders + (orders >= own_index).astype(jnp.int32)).astype(jnp.int32)


def with_ends(values, stream_key, low, largest):
    spot = [jax.random.randint(jax.random.fold_in(stream_key, axis), (), 0, length) for axis, length in enumerate(values.shape)]
    widest = values.shape.index(max(values.shape))
    beside = spot[:widest] + [(spot[widest] + 1) % values.shape[widest]] + spot[widest + 1:]
    return values.at[tuple(spot)].set(low).at[tuple(beside)].set(largest)


def levels(own_key, dims, cuts, low, top_value):
    factor_of = 1.0
    for position, parts in cuts:
        draws = jax.random.uniform(jax.random.fold_in(jax.random.fold_in(own_key, 6), position), (parts,), jnp.float32, low / len(cuts), top_value / len(cuts))
        factor_of = factor_of * jnp.repeat(jnp.exp(draws), dims[position] // parts).reshape((-1,) + (1,) * (len(dims) - 1 - position))
    return factor_of


def deal_out(rng, own, number, rows, count, top, reach, skew):
    order = jax.random.permutation(rng, count)
    crowded, ordinary = shares(count, rows * top, reach, skew, True), shares(count, rows * top, reach, skew, False)
    places = jnp.arange(count)

    def named(lengths, turn):
        used = int((lengths > 0).sum())
        fixed = max(1, used // 4)
        shifted = fixed + (places - fixed + turn * (used - fixed)) % max(1, count - fixed)
        return jnp.zeros((count,), jnp.int32).at[order[jnp.where(places < fixed, places, shifted)]].set(jnp.asarray(lengths, jnp.int32))

    lengths = jnp.where(number % 4 == 0, named(crowded, number // 4), named(ordinary, number - number // 4 - 1))
    mixed = jax.random.permutation(jax.random.fold_in(own, 3), count)
    donor, taker = mixed[0:count // 2 * 2:2], mixed[1:count // 2 * 2:2]
    room = jnp.minimum(lengths[donor] - 1, reach - lengths[taker]) // 2
    room = jnp.where((donor == order[0]) | (taker == order[0]) | (lengths[taker] == 0), 0, jnp.maximum(room, 0))
    shifted = jax.random.randint(jax.random.fold_in(own, 4), (count // 2,), 0, 1 << 20) % (room + 1)
    lengths = lengths.at[donor].add(-shifted).at[taker].add(shifted)
    labels = jnp.searchsorted(jnp.cumsum(lengths), jnp.arange(rows * top), side="right").astype(jnp.int32)
    table = labels.reshape(top, rows).T
    table = table[jax.random.permutation(jax.random.fold_in(own, 1), rows)]
    turn = jax.random.randint(jax.random.fold_in(own, 2), (rows, 1), 0, top)
    return jnp.take_along_axis(table, (jnp.arange(top)[None, :] + turn) % top, axis=1)


def shares(number_of, total, limit, skew, full):
    portions = [(1 << 20) // math.isqrt(grade ** skew) + 1 for grade in range(1, number_of + 1)]
    largest = limit if full else min(limit, max(-(-total // number_of), total * portions[0] // sum(portions)))
    least = 1 if total - largest >= number_of - 1 else 0
    holding, surplus = [largest] + [least] * (number_of - 1), total - largest - least * (number_of - 1)
    while surplus > 0:
        free = [i for i in range(1, number_of) if holding[i] < largest] or [i for i in range(1, number_of) if holding[i] < limit]
        whole, budget = sum([portions[i] for i in free]), surplus
        for i in free:
            addition = min(limit - holding[i], max(1, budget * portions[i] // whole), surplus)
            holding[i] = holding[i] + addition
            surplus = surplus - addition
    return np.array(holding)


def normal_values(stream_key, extent, scale, bound, cuts=(), kind=jnp.bfloat16):
    level = levels(stream_key, extent, cuts, -0.22, 0.18) if cuts else 1.0
    values = jax.random.normal(stream_key, extent, jnp.float32) * scale * level
    return jnp.minimum(jnp.maximum(values, -bound), bound).astype(kind)


def setup_inputs(seed: int = 0) -> dict:
    key_list = jax.random.split(jax.random.key(seed), 8)
    fields = normal_values(key_list[0], (SAMPLES, NLOC), 1.0, 6.0, ((0, 8), (1, 4)))
    near_coef = normal_values(key_list[1], (NBLK, NEAR, BLOCK, BLOCK), (BLOCK * (NEAR + FAR)) ** -0.5, 0.25, ((0, 32),))
    far_coef = normal_values(key_list[2], (NBLK, FAR, BLOCK, BLOCK), (BLOCK * (NEAR + FAR)) ** -0.5, 0.25, ((0, 32),))
    inv_factor = draw_inv_factor(jax.random.fold_in(key_list[7], 71), 0)
    near_block = draw_near_block(jax.random.fold_in(key_list[7], 71), 0)
    far_region_keys = jax.random.split(jax.random.fold_in(key_list[5], 1), NBLK // BLK_DEV)
    far_region_turns = jax.random.permutation(jax.random.fold_in(key_list[5], 3), NBLK // BLK_DEV)
    far_region = jax.vmap(lambda own, number: deal_out(jax.random.fold_in(key_list[5], 2), own, number, BLK_DEV, N_REGION, FAR, CAP, 2))(far_region_keys, far_region_turns).reshape((NBLK, FAR))
    far_block = with_ends(jax.random.randint(key_list[6], (NBLK, FAR), 0, BLK_DEV), jax.random.fold_in(key_list[6], 1), 0, BLK_DEV - 1).astype(jnp.int32)
    return {"fields": fields, "near_coef": near_coef, "far_coef": far_coef, "inv_factor": inv_factor, "near_block": near_block, "far_region": far_region, "far_block": far_block}


def reference(fields, near_coef, far_coef, inv_factor, near_block, far_region, far_block):
    field_blocks = fields.reshape(SAMPLES, NBLK, BLOCK)
    block_ids = jnp.arange(NBLK, dtype=jnp.int32)
    group_of = block_ids // BLK_DEV
    near_ids = (group_of * BLK_DEV)[:, None] + near_block
    shard_of = group_of % N_SHARD
    far_ids = (far_region * N_SHARD + shard_of[:, None]) * BLK_DEV + far_block

    def one_group(group):
        start = (group * BLK_DEV).astype(jnp.int32)
        near_rows = lax.dynamic_slice_in_dim(near_ids, start, BLK_DEV, 0).reshape(-1).astype(jnp.int32)
        far_rows = lax.dynamic_slice_in_dim(far_ids, start, BLK_DEV, 0).reshape(-1).astype(jnp.int32)
        near_vals = jnp.take(field_blocks, near_rows, axis=1).reshape(SAMPLES, BLK_DEV, NEAR, BLOCK)
        far_vals = jnp.take(field_blocks, far_rows, axis=1).reshape(SAMPLES, BLK_DEV, FAR, BLOCK)
        own_vals = lax.dynamic_slice_in_dim(field_blocks, start, BLK_DEV, 1)
        near_here = lax.dynamic_slice_in_dim(near_coef, start, BLK_DEV, 0)
        far_here = lax.dynamic_slice_in_dim(far_coef, start, BLK_DEV, 0)
        factor_here = lax.dynamic_slice_in_dim(inv_factor, start, BLK_DEV, 0)
        cond_mean = jnp.einsum("sbjd,bjde->sbe", near_vals.astype(jnp.float32), near_here.astype(jnp.float32))
        cond_mean = cond_mean + jnp.einsum("sbjd,bjde->sbe", far_vals.astype(jnp.float32), far_here.astype(jnp.float32))
        residual = (own_vals.astype(jnp.float32) - cond_mean).astype(jnp.bfloat16)
        result = jnp.einsum("sbd,bde->sbe", residual.astype(jnp.float32), factor_here.astype(jnp.float32))
        return result.astype(jnp.bfloat16)

    grouped = lax.map(one_group, jnp.arange(NBLK // BLK_DEV, dtype=jnp.int32))
    return jnp.transpose(grouped, (1, 0, 2, 3)).reshape(SAMPLES, NLOC)
```

```python
import functools

import jax
import jax.numpy as jnp
from jax import lax
from jax.experimental import pallas as pl
from jax.experimental.pallas import tpu as pltpu
from jax.sharding import PartitionSpec as P

CORES = 2
MESH = pl.DeviceIdType.MESH


def kernel(regions, shards, fields, near_coef, far_coef, inv_factor, near_list,
           region_list, block_list, out, held, land, near_w, far_w, inv_w, stage,
           near_0, region_0, block_0, near_1, region_1, block_1,
           load_sem, ready, gather_send, gather_recv, weight_send, weight_recv,
           land_send, land_recv, back_send, back_recv):
    blocks, rows, width = held.shape[2:]
    near, far = near_coef.shape[1], far_coef.shape[1]
    members = shards * rows
    chips = regions // CORES
    r, s = lax.axis_index("region"), lax.axis_index("shard")
    core = lax.rem(r, CORES)
    pair = lax.div(r, CORES)
    lead, mate = core == CORES - 1, core == 0
    order = list(reversed(range(1, shards)))

    def odd_of(k):
        return lax.rem(pair + k, chips) * CORES + CORES - 1

    def wait_for(ref, sem):
        pltpu.make_async_copy(ref, ref, sem).wait()

    def send(src, dst, send_sem, recv_sem, to):
        pltpu.make_async_remote_copy(
            src_ref=src, dst_ref=dst, send_sem=send_sem, recv_sem=recv_sem,
            device_id=to, device_id_type=MESH).start()

    barrier = pltpu.get_barrier_semaphore()
    load = pltpu.make_async_copy(fields, held.at[r], load_sem.at[0])
    weights = [(near_coef, near_w, weight_recv.at[0]), (far_coef, far_w, weight_recv.at[1]),
               (inv_factor, inv_w, weight_recv.at[2])]
    lists = [(near_list, near_0, near_1, weight_recv.at[3]),
             (region_list, region_0, region_1, weight_recv.at[4]),
             (block_list, block_0, block_1, weight_recv.at[5])]
    local = [pltpu.make_async_copy(a, b.at[1], load_sem.at[1 + i])
             for i, (a, b, _) in enumerate(weights)]
    local += [pltpu.make_async_copy(a, b, load_sem.at[4 + i])
              for i, (a, _, b, _) in enumerate(lists)]

    @pl.when(lead)
    def _():
        for w in order:
            pl.semaphore_signal(barrier, inc=1, device_id=(r, s ^ w), device_id_type=MESH)
        for k in range(chips):
            pl.semaphore_signal(
                barrier, inc=1, device_id=(lax.rem(pair + k, chips) * CORES, s),
                device_id_type=MESH)
        load.start()

    @pl.when(mate)
    def _():
        load.start()
        pl.semaphore_wait(barrier, chips)
        pl.semaphore_signal(ready, inc=1, device_id=(r + 1, s), device_id_type=MESH)
        load.wait()
        for k in reversed(range(chips)):
            send(held.at[r], held.at[r], gather_send.at[0], gather_recv, (odd_of(k), s))
        mine = (r + 1, s)
        for a, b, _, sem in lists:
            send(a, b, weight_send.at[0], sem, mine)
        for a, b, sem in weights:
            send(a, b.at[0], weight_send.at[0], sem, mine)
        for k in range(chips):
            wait_for(held.at[r], gather_send.at[0])
        for a, b, _, sem in lists:
            wait_for(a, weight_send.at[0])
        for a, b, sem in weights:
            wait_for(a, weight_send.at[0])
        wait_for(out, back_recv)

    @pl.when(lead)
    def _():
        for copy in local:
            copy.start()
        load.wait()
        pl.semaphore_wait(ready, 1)
        for k in range(1, chips):
            send(held.at[r], held.at[r], gather_send.at[0], gather_recv, (odd_of(k), s))
        wait_for(held.at[pl.ds(0, regions - 1)], gather_recv)
        pl.semaphore_wait(barrier, shards - 1)
        for w in order:
            send(held.at[:, s ^ w], land.at[:, :, s], land_send, land_recv, (r, s ^ w))
        own = pltpu.make_async_copy(held.at[:, s], land.at[:, :, s], load_sem.at[0])
        own.start()
        for copy in local:
            copy.wait()
        for a, b, _, sem in lists:
            wait_for(b, sem)
        for a, b, sem in weights:
            wait_for(b.at[0], sem)
        own.wait()
        wait_for(held.at[:, pl.ds(0, shards - 1)], land_recv)

        for half, (near_i, region_i, block_i) in enumerate(
                ((near_0, region_0, block_0), (near_1, region_1, block_1))):
            here = r - 1 + half
            for b in range(blocks):
                x = [land[here, near_i[b, j]] for j in range(near)]
                x += [land[region_i[j, b], block_i[j, b]] for j in range(far)]
                x = jnp.concatenate([v.reshape(members, width) for v in x], axis=1)
                mean = jnp.dot(x[:, :near * width], near_w[half, b].reshape(near * width, width),
                               preferred_element_type=jnp.float32)
                mean += jnp.dot(x[:, near * width:], far_w[half, b].reshape(far * width, width),
                                preferred_element_type=jnp.float32)
                mine = land[here, b].reshape(members, width).astype(jnp.float32)
                white = jnp.dot((mine - mean).astype(jnp.bfloat16), inv_w[half, b],
                                preferred_element_type=jnp.float32)
                stage[half, :, b] = white.astype(jnp.bfloat16).reshape(shards, rows, width)
            for w in order:
                send(stage.at[half, s ^ w], out.at[s], back_send, back_recv, (here, s ^ w))
            if half == 0:
                send(stage.at[half, s], out.at[s], back_send, back_recv, (here, s))
            else:
                pltpu.make_async_copy(stage.at[half, s], out.at[s], back_recv).start()

        for k in range(1, chips):
            wait_for(held.at[r], gather_send.at[0])
        wait_for(held.at[:, pl.ds(0, shards - 1)], land_send)
        wait_for(stage.at[0], back_send)
        wait_for(stage.at[1, pl.ds(0, shards - 1)], back_send)
        wait_for(out, back_recv)


def body(fields, near_coef, far_coef, inv_factor, near_block, far_region, far_block):
    shards, regions = lax.axis_size("shard"), lax.axis_size("region")
    rows, columns = fields.shape
    blocks, width = near_coef.shape[0], near_coef.shape[3]
    tiles = columns // width
    tiled = jnp.transpose(fields.reshape(rows, tiles, width), (1, 0, 2))
    tiled = tiled.reshape(shards, blocks, rows, width)
    hbm = pl.BlockSpec(memory_space=pl.ANY)
    half = jnp.bfloat16
    white = pl.pallas_call(
        functools.partial(kernel, regions, shards),
        out_shape=pltpu.VMEM(tiled.shape, half),
        in_specs=[hbm] * 7,
        out_specs=pl.BlockSpec(memory_space=pltpu.VMEM),
        scratch_shapes=[
            pltpu.VMEM((regions, shards, blocks, rows, width), half),
            pltpu.VMEM((regions, blocks, shards, rows, width), half),
            pltpu.VMEM((CORES, *near_coef.shape), half),
            pltpu.VMEM((CORES, *far_coef.shape), half),
            pltpu.VMEM((CORES, *inv_factor.shape), half),
            pltpu.VMEM((CORES, shards, blocks, rows, width), half),
        ] + [pltpu.SMEM(a.shape, jnp.int32) for a in (near_block, far_region.T, far_block.T)] * 2 + [
            pltpu.SemaphoreType.DMA((7,)),
            pltpu.SemaphoreType.REGULAR,
            pltpu.SemaphoreType.DMA((1,)),
            pltpu.SemaphoreType.DMA,
            pltpu.SemaphoreType.DMA((1,)),
            pltpu.SemaphoreType.DMA((6,)),
            pltpu.SemaphoreType.DMA,
            pltpu.SemaphoreType.DMA,
            pltpu.SemaphoreType.DMA,
            pltpu.SemaphoreType.DMA,
        ],
        compiler_params=pltpu.CompilerParams(collective_id=0, has_side_effects=True),
    )(tiled, near_coef, far_coef, inv_factor, near_block, far_region.T, far_block.T)
    white = white.reshape(tiles, rows, width)
    return jnp.transpose(white, (1, 0, 2)).reshape(rows, columns)


def solution(mesh):
    return jax.shard_map(
        body,
        mesh=mesh,
        in_specs=(
            P("shard", "region"),
            P(("region", "shard"), None, None, None),
            P(("region", "shard"), None, None, None),
            P(("region", "shard"), None, None),
            P(("region", "shard"), None),
            P(("region", "shard"), None),
            P(("region", "shard"), None),
        ),
        out_specs=P("shard", "region"),
        check_vma=False,
    )
```

```python
import functools

import jax
import jax.numpy as jnp
from jax import lax
from jax.experimental import pallas as pl
from jax.experimental.pallas import tpu as pltpu
from jax.sharding import PartitionSpec as P

CORES = 2
MESH = pl.DeviceIdType.MESH


def kernel(regions, shards, fields, near_coef, far_coef, inv_factor, near_list,
           region_list, block_list, out, held, first, rest, near_w, far_w, inv_w, stage,
           near_0, region_0, block_0, near_1, region_1, block_1,
           load_sem, ready, gather_send, gather_recv, weight_send, weight_recv,
           land_send, land_recv, back_send, back_recv):
    blocks, rows, width = held.shape[2:]
    near, far = near_coef.shape[1], far_coef.shape[1]
    members = shards * rows
    chips = regions // CORES
    r, s = lax.axis_index("region"), lax.axis_index("shard")
    core = lax.rem(r, CORES)
    pair = lax.div(r, CORES)
    lead, mate = core == CORES - 1, core == 0
    order = list(reversed(range(1, shards)))

    def odd_of(k):
        return lax.rem(pair + k, chips) * CORES + CORES - 1

    def wait_for(ref, sem):
        pltpu.make_async_copy(ref, ref, sem).wait()

    def send(src, dst, send_sem, recv_sem, to):
        pltpu.make_async_remote_copy(
            src_ref=src, dst_ref=dst, send_sem=send_sem, recv_sem=recv_sem,
            device_id=to, device_id_type=MESH).start()

    barrier = pltpu.get_barrier_semaphore()
    load = pltpu.make_async_copy(fields, held.at[r], load_sem.at[0])
    weights = [(near_coef, near_w, weight_recv.at[0]), (far_coef, far_w, weight_recv.at[1]),
               (inv_factor, inv_w, weight_recv.at[2])]
    lists = [(near_list, near_0, near_1, weight_recv.at[3]),
             (region_list, region_0, region_1, weight_recv.at[4]),
             (block_list, block_0, block_1, weight_recv.at[5])]
    local = [pltpu.make_async_copy(a, b.at[1], load_sem.at[1 + i])
             for i, (a, b, _) in enumerate(weights)]
    local += [pltpu.make_async_copy(a, b, load_sem.at[4 + i])
              for i, (a, _, b, _) in enumerate(lists)]

    @pl.when(lead)
    def _():
        for w in order:
            pl.semaphore_signal(barrier, inc=1, device_id=(r, s ^ w), device_id_type=MESH)
        for k in range(chips):
            pl.semaphore_signal(
                barrier, inc=1, device_id=(lax.rem(pair + k, chips) * CORES, s),
                device_id_type=MESH)
        load.start()

    @pl.when(mate)
    def _():
        pl.semaphore_wait(barrier, chips)
        for k in reversed(range(chips)):
            send(fields, held.at[r], gather_send.at[0], gather_recv, (odd_of(k), s))
        pl.semaphore_signal(ready, inc=1, device_id=(r + 1, s), device_id_type=MESH)
        mine = (r + 1, s)
        for a, b, _, sem in lists:
            send(a, b, weight_send.at[0], sem, mine)
        for a, b, sem in weights:
            send(a, b.at[0], weight_send.at[0], sem, mine)
        for k in range(chips):
            wait_for(held.at[r], gather_send.at[0])
        for a, b, _, sem in lists:
            wait_for(a, weight_send.at[0])
        for a, b, sem in weights:
            wait_for(a, weight_send.at[0])
        wait_for(out, back_recv)

    @pl.when(lead)
    def _():
        for copy in local:
            copy.start()
        load.wait()
        pl.semaphore_wait(ready, 1)
        for k in range(1, chips):
            send(held.at[r], held.at[r], gather_send.at[0], gather_recv, (odd_of(k), s))
        wait_for(held.at[pl.ds(0, regions - 1)], gather_recv)
        pl.semaphore_wait(barrier, shards - 1)
        def spread(dst):
            for w in order:
                send(held.at[:, s ^ w], dst, land_send, land_recv.at[s], (r, s ^ w))
            pltpu.make_async_copy(held.at[:, s], dst, land_recv.at[s]).start()

        @pl.when(s == 0)
        def _():
            spread(first)

        @pl.when(s > 0)
        def _():
            spread(rest.at[:, :, s - 1])

        for copy in local:
            copy.wait()
        for a, b, _, sem in lists:
            wait_for(b, sem)
        for a, b, sem in weights:
            wait_for(b.at[0], sem)

        indices = ((near_0, region_0, block_0), (near_1, region_1, block_1))

        def whiten(half, ref, start, count):
            near_i, region_i, block_i = indices[half]
            here = r - 1 + half
            for b in range(blocks):
                x = [ref[here, near_i[b, j]] for j in range(near)]
                x += [ref[region_i[j, b], block_i[j, b]] for j in range(far)]
                x = jnp.concatenate([v.reshape(count * rows, width) for v in x], axis=1)
                mean = jnp.dot(x[:, :near * width], near_w[half, b].reshape(near * width, width),
                               preferred_element_type=jnp.float32)
                mean += jnp.dot(x[:, near * width:], far_w[half, b].reshape(far * width, width),
                                preferred_element_type=jnp.float32)
                mine = ref[here, b].reshape(count * rows, width).astype(jnp.float32)
                white = jnp.dot((mine - mean).astype(jnp.bfloat16), inv_w[half, b],
                                preferred_element_type=jnp.float32)
                white = white.astype(jnp.bfloat16).reshape(count, rows, width)
                stage[half, pl.ds(start, count), b] = white
            for k in range(start, start + count):
                if half == 0:
                    send(stage.at[half, k], out.at[s], back_send, back_recv, (here, k))
                else:
                    @pl.when(s != k)
                    def _():
                        send(stage.at[half, k], out.at[s], back_send, back_recv, (here, k))

                    @pl.when(s == k)
                    def _():
                        pltpu.make_async_copy(stage.at[half, k], out.at[s], back_recv).start()

        part = held.at[:, 0]
        wait_for(part, land_recv.at[0])
        whiten(0, first, 0, 1)
        whiten(1, first, 0, 1)
        for k in range(1, shards):
            wait_for(part, land_recv.at[k])
        whiten(0, rest, 1, shards - 1)
        whiten(1, rest, 1, shards - 1)

        for k in range(1, chips):
            wait_for(held.at[r], gather_send.at[0])
        wait_for(held.at[:, pl.ds(0, shards - 1)], land_send)
        wait_for(stage.at[0], back_send)
        wait_for(stage.at[1, pl.ds(0, shards - 1)], back_send)
        wait_for(out, back_recv)


def body(fields, near_coef, far_coef, inv_factor, near_block, far_region, far_block):
    shards, regions = lax.axis_size("shard"), lax.axis_size("region")
    rows, columns = fields.shape
    blocks, width = near_coef.shape[0], near_coef.shape[3]
    tiles = columns // width
    tiled = jnp.transpose(fields.reshape(rows, tiles, width), (1, 0, 2))
    tiled = tiled.reshape(shards, blocks, rows, width)
    hbm = pl.BlockSpec(memory_space=pl.ANY)
    half = jnp.bfloat16
    white = pl.pallas_call(
        functools.partial(kernel, regions, shards),
        out_shape=pltpu.VMEM(tiled.shape, half),
        in_specs=[hbm] * 7,
        out_specs=pl.BlockSpec(memory_space=pltpu.VMEM),
        scratch_shapes=[
            pltpu.VMEM((regions, shards, blocks, rows, width), half),
            pltpu.VMEM((regions, blocks, rows, width), half),
            pltpu.VMEM((regions, blocks, shards - 1, rows, width), half),
            pltpu.VMEM((CORES, *near_coef.shape), half),
            pltpu.VMEM((CORES, *far_coef.shape), half),
            pltpu.VMEM((CORES, *inv_factor.shape), half),
            pltpu.VMEM((CORES, shards, blocks, rows, width), half),
        ] + [pltpu.SMEM(a.shape, jnp.int32) for a in (near_block, far_region.T, far_block.T)] * 2 + [
            pltpu.SemaphoreType.DMA((7,)),
            pltpu.SemaphoreType.REGULAR,
            pltpu.SemaphoreType.DMA((1,)),
            pltpu.SemaphoreType.DMA,
            pltpu.SemaphoreType.DMA((1,)),
            pltpu.SemaphoreType.DMA((6,)),
            pltpu.SemaphoreType.DMA,
            pltpu.SemaphoreType.DMA((shards,)),
            pltpu.SemaphoreType.DMA,
            pltpu.SemaphoreType.DMA,
        ],
        compiler_params=pltpu.CompilerParams(collective_id=0, has_side_effects=True),
    )(tiled, near_coef, far_coef, inv_factor, near_block, far_region.T, far_block.T)
    white = white.reshape(tiles, rows, width)
    return jnp.transpose(white, (1, 0, 2)).reshape(rows, columns)


def solution(mesh):
    return jax.shard_map(
        body,
        mesh=mesh,
        in_specs=(
            P("shard", "region"),
            P(("region", "shard"), None, None, None),
            P(("region", "shard"), None, None, None),
            P(("region", "shard"), None, None),
            P(("region", "shard"), None),
            P(("region", "shard"), None),
            P(("region", "shard"), None),
        ),
        out_specs=P("shard", "region"),
        check_vma=False,
    )
```

```python
import functools

import jax
import jax.numpy as jnp
from jax import lax
from jax.experimental import pallas as pl
from jax.experimental.pallas import tpu as pltpu
from jax.sharding import PartitionSpec as P

CORES = 2
MESH = pl.DeviceIdType.MESH


def kernel(regions, shards, fields, near_coef, far_coef, inv_factor, near_list,
           region_list, block_list, out, held, first, rest, coef_w, inv_w, stage,
           near_0, region_0, block_0, near_1, region_1, block_1,
           load_sem, ready, gather_send, gather_recv, weight_send, weight_recv,
           land_send, land_recv, back_send, back_recv):
    blocks, rows, width = held.shape[2:]
    near, far = near_coef.shape[1], far_coef.shape[1]
    members = shards * rows
    chips = regions // CORES
    r, s = lax.axis_index("region"), lax.axis_index("shard")
    core = lax.rem(r, CORES)
    pair = lax.div(r, CORES)
    lead, mate = core == CORES - 1, core == 0
    order = list(reversed(range(1, shards)))

    def odd_of(k):
        return lax.rem(pair + k, chips) * CORES + CORES - 1

    def wait_for(ref, sem):
        pltpu.make_async_copy(ref, ref, sem).wait()

    def send(src, dst, send_sem, recv_sem, to):
        pltpu.make_async_remote_copy(
            src_ref=src, dst_ref=dst, send_sem=send_sem, recv_sem=recv_sem,
            device_id=to, device_id_type=MESH).start()

    barrier = pltpu.get_barrier_semaphore()
    load = pltpu.make_async_copy(fields, held.at[r], load_sem.at[0])
    weights = [(near_coef, coef_w.at[:, :, pl.ds(0, near)], weight_recv.at[0]),
               (far_coef, coef_w.at[:, :, pl.ds(near, far)], weight_recv.at[1]),
               (inv_factor, inv_w, weight_recv.at[2])]
    lists = [(near_list, near_0, near_1, weight_recv.at[3]),
             (region_list, region_0, region_1, weight_recv.at[4]),
             (block_list, block_0, block_1, weight_recv.at[5])]
    local = [pltpu.make_async_copy(a, b.at[1], load_sem.at[1 + i])
             for i, (a, b, _) in enumerate(weights)]
    local += [pltpu.make_async_copy(a, b, load_sem.at[4 + i])
              for i, (a, _, b, _) in enumerate(lists)]

    @pl.when(lead)
    def _():
        for w in order:
            pl.semaphore_signal(barrier, inc=1, device_id=(r, s ^ w), device_id_type=MESH)
        for k in range(chips):
            pl.semaphore_signal(
                barrier, inc=1, device_id=(lax.rem(pair + k, chips) * CORES, s),
                device_id_type=MESH)
        load.start()

    @pl.when(mate)
    def _():
        pl.semaphore_wait(barrier, chips)
        for k in reversed(range(chips)):
            send(fields, held.at[r], gather_send.at[0], gather_recv, (odd_of(k), s))
        pl.semaphore_signal(ready, inc=1, device_id=(r + 1, s), device_id_type=MESH)
        mine = (r + 1, s)
        for a, b, _, sem in lists:
            send(a, b, weight_send.at[0], sem, mine)
        for a, b, sem in weights:
            send(a, b.at[0], weight_send.at[0], sem, mine)
        for k in range(chips):
            wait_for(held.at[r], gather_send.at[0])
        for a, b, _, sem in lists:
            wait_for(a, weight_send.at[0])
        for a, b, sem in weights:
            wait_for(a, weight_send.at[0])
        wait_for(out, back_recv)

    @pl.when(lead)
    def _():
        for copy in local:
            copy.start()
        load.wait()
        pl.semaphore_wait(ready, 1)
        for k in range(1, chips):
            send(held.at[r], held.at[r], gather_send.at[0], gather_recv, (odd_of(k), s))
        wait_for(held.at[pl.ds(0, regions - 1)], gather_recv)
        pl.semaphore_wait(barrier, shards - 1)
        def spread(dst):
            for w in order:
                send(held.at[:, s ^ w], dst, land_send, land_recv.at[s], (r, s ^ w))
            pltpu.make_async_copy(held.at[:, s], dst, land_recv.at[s]).start()

        @pl.when(s == 0)
        def _():
            spread(first)

        @pl.when(s > 0)
        def _():
            spread(rest.at[:, :, s - 1])

        for copy in local:
            copy.wait()
        for a, b, _, sem in lists:
            wait_for(b, sem)
        for a, b, sem in weights:
            wait_for(b.at[0], sem)

        indices = ((near_0, region_0, block_0), (near_1, region_1, block_1))

        def residuals(half, ref, count):
            near_i, region_i, block_i = indices[half]
            here = r - 1 + half
            left = []
            for b in range(blocks):
                x = [ref[here, near_i[b, j]] for j in range(near)]
                x += [ref[region_i[j, b], block_i[j, b]] for j in range(far)]
                x = jnp.concatenate([v.reshape(count * rows, width) for v in x], axis=1)
                mean = jnp.dot(x, coef_w[half, b].reshape((near + far) * width, width),
                               preferred_element_type=jnp.float32)
                mine = ref[here, b].reshape(count * rows, width).astype(jnp.float32)
                left.append((mine - mean).astype(jnp.bfloat16))
            return left

        def give_back(half, left, start, count):
            here = r - 1 + half
            for b in range(blocks):
                white = jnp.dot(left[b], inv_w[half, b], preferred_element_type=jnp.float32)
                white = white.astype(jnp.bfloat16).reshape(count, rows, width)
                stage[half, pl.ds(start, count), b] = white
            for k in range(start, start + count):
                if half == 0:
                    send(stage.at[half, k], out.at[s], back_send, back_recv, (here, k))
                else:
                    @pl.when(s != k)
                    def _():
                        send(stage.at[half, k], out.at[s], back_send, back_recv, (here, k))

                    @pl.when(s == k)
                    def _():
                        pltpu.make_async_copy(stage.at[half, k], out.at[s], back_recv).start()

        def whiten(ref, start, count):
            for half in range(CORES):
                give_back(half, residuals(half, ref, count), start, count)

        part = held.at[:, 0]
        wait_for(part, land_recv.at[0])
        whiten(first, 0, 1)
        for k in range(1, shards):
            wait_for(part, land_recv.at[k])
        whiten(rest, 1, shards - 1)

        for k in range(1, chips):
            wait_for(held.at[r], gather_send.at[0])
        wait_for(held.at[:, pl.ds(0, shards - 1)], land_send)
        wait_for(stage.at[0], back_send)
        wait_for(stage.at[1, pl.ds(0, shards - 1)], back_send)
        wait_for(out, back_recv)


def body(fields, near_coef, far_coef, inv_factor, near_block, far_region, far_block):
    shards, regions = lax.axis_size("shard"), lax.axis_size("region")
    rows, columns = fields.shape
    blocks, width = near_coef.shape[0], near_coef.shape[3]
    tiles = columns // width
    tiled = jnp.transpose(fields.reshape(rows, tiles, width), (1, 0, 2))
    tiled = tiled.reshape(shards, blocks, rows, width)
    hbm = pl.BlockSpec(memory_space=pl.ANY)
    half = jnp.bfloat16
    white = pl.pallas_call(
        functools.partial(kernel, regions, shards),
        out_shape=pltpu.VMEM(tiled.shape, half),
        in_specs=[hbm] * 7,
        out_specs=pl.BlockSpec(memory_space=pltpu.VMEM),
        scratch_shapes=[
            pltpu.VMEM((regions, shards, blocks, rows, width), half),
            pltpu.VMEM((regions, blocks, rows, width), half),
            pltpu.VMEM((regions, blocks, shards - 1, rows, width), half),
            pltpu.VMEM((CORES, blocks, near_coef.shape[1] + far_coef.shape[1], width, width), half),
            pltpu.VMEM((CORES, *inv_factor.shape), half),
            pltpu.VMEM((CORES, shards, blocks, rows, width), half),
        ] + [pltpu.SMEM(a.shape, jnp.int32) for a in (near_block, far_region.T, far_block.T)] * 2 + [
            pltpu.SemaphoreType.DMA((7,)),
            pltpu.SemaphoreType.REGULAR,
            pltpu.SemaphoreType.DMA((1,)),
            pltpu.SemaphoreType.DMA,
            pltpu.SemaphoreType.DMA((1,)),
            pltpu.SemaphoreType.DMA((6,)),
            pltpu.SemaphoreType.DMA,
            pltpu.SemaphoreType.DMA((shards,)),
            pltpu.SemaphoreType.DMA,
            pltpu.SemaphoreType.DMA,
        ],
        compiler_params=pltpu.CompilerParams(collective_id=0, has_side_effects=True),
    )(tiled, near_coef, far_coef, inv_factor, near_block, far_region.T, far_block.T)
    white = white.reshape(tiles, rows, width)
    return jnp.transpose(white, (1, 0, 2)).reshape(rows, columns)


def solution(mesh):
    return jax.shard_map(
        body,
        mesh=mesh,
        in_specs=(
            P("shard", "region"),
            P(("region", "shard"), None, None, None),
            P(("region", "shard"), None, None, None),
            P(("region", "shard"), None, None),
            P(("region", "shard"), None),
            P(("region", "shard"), None),
            P(("region", "shard"), None),
        ),
        out_specs=P("shard", "region"),
        check_vma=False,
    )
```

```python
import functools

import jax
import jax.numpy as jnp
from jax import lax
from jax.experimental import pallas as pl
from jax.experimental.pallas import tpu as pltpu
from jax.sharding import PartitionSpec as P

CORES = 2
RELAY = 1
MESH = pl.DeviceIdType.MESH


def kernel(regions, shards, fields, near_coef, far_coef, inv_factor, near_list,
           region_list, block_list, out, held, relay, first, second, third, coef_w, inv_w, stage,
           near_0, region_0, block_0, near_1, region_1, block_1,
           load_sem, ready, gather_send, gather_recv, weight_send, weight_recv,
           land_send, land_recv, back_send, back_recv, relay_send, relay_recv):
    blocks, rows, width = held.shape[2:]
    near, far = near_coef.shape[1], far_coef.shape[1]
    members = shards * rows
    chips = regions // CORES
    r, s = lax.axis_index("region"), lax.axis_index("shard")
    core = lax.rem(r, CORES)
    pair = lax.div(r, CORES)
    lead, mate = core == CORES - 1, core == 0
    order = list(reversed(range(1, shards)))
    last = shards - 1
    starts = (0, 1, shards // 2, shards)
    relays, fed = (s == RELAY) & (pair == 0), s == 0
    via = (CORES - 1, RELAY)

    def odd_of(k):
        return lax.rem(pair + k, chips) * CORES + CORES - 1

    def wait_for(ref, sem):
        pltpu.make_async_copy(ref, ref, sem).wait()

    def send(src, dst, send_sem, recv_sem, to):
        pltpu.make_async_remote_copy(
            src_ref=src, dst_ref=dst, send_sem=send_sem, recv_sem=recv_sem,
            device_id=to, device_id_type=MESH).start()

    barrier = pltpu.get_barrier_semaphore()
    load = pltpu.make_async_copy(fields, held.at[r], load_sem.at[0])
    weights = [(near_coef, coef_w.at[:, :, pl.ds(0, near)], weight_recv.at[0]),
               (far_coef, coef_w.at[:, :, pl.ds(near, far)], weight_recv.at[1]),
               (inv_factor, inv_w, weight_recv.at[2])]
    lists = [(near_list, near_0, near_1, weight_recv.at[3]),
             (region_list, region_0, region_1, weight_recv.at[4]),
             (block_list, block_0, block_1, weight_recv.at[5])]
    local = [pltpu.make_async_copy(a, b.at[1], load_sem.at[1 + i])
             for i, (a, b, _) in enumerate(weights)]
    local += [pltpu.make_async_copy(a, b, load_sem.at[4 + i])
              for i, (a, _, b, _) in enumerate(lists)]

    def greet(to):
        pl.semaphore_signal(barrier, inc=1, device_id=to, device_id_type=MESH)

    @pl.when(lead)
    def _():
        @pl.when(relays)
        def _():
            for k in reversed(range(chips)):
                greet((k * CORES, 0))

        for w in order:
            greet((r, s ^ w))
        for k in range(chips):
            greet((lax.rem(pair + k, chips) * CORES, s))
        load.start()

    @pl.when(mate & fed)
    def _():
        load.start()
        pl.semaphore_wait(barrier, chips + 1)
        load.wait()
        send(held.at[r, last], relay.at[r], relay_send, relay_recv, via)
        pl.semaphore_signal(ready, inc=1, device_id=(r + 1, s), device_id_type=MESH)
        for k in reversed(range(chips)):
            send(held.at[r], held.at[r], gather_send.at[0], gather_recv, (odd_of(k), s))


    @pl.when(mate & (s > 0))
    def _():
        pl.semaphore_wait(barrier, chips)
        for k in reversed(range(chips)):
            send(fields, held.at[r], gather_send.at[0], gather_recv, (odd_of(k), s))
        pl.semaphore_signal(ready, inc=1, device_id=(r + 1, s), device_id_type=MESH)

    @pl.when(mate)
    def _():
        mine = (r + 1, s)
        for a, b, _, sem in lists:
            send(a, b, weight_send.at[0], sem, mine)
        for a, b, sem in weights:
            send(a, b.at[0], weight_send.at[0], sem, mine)
        for k in range(chips):
            wait_for(held.at[r], gather_send.at[0])
        for a, b, _, sem in lists:
            wait_for(a, weight_send.at[0])
        for a, b, sem in weights:
            wait_for(a, weight_send.at[0])

        @pl.when(fed)
        def _():
            wait_for(relay.at[0], relay_send)

        wait_for(out, back_recv)

    @pl.when(lead)
    def _():
        for copy in local:
            copy.start()
        load.wait()
        pl.semaphore_wait(ready, 1)

        @pl.when(fed)
        def _():
            send(held.at[r, last], relay.at[r], relay_send, relay_recv, via)

        for k in range(1, chips):
            send(held.at[r], held.at[r], gather_send.at[0], gather_recv, (odd_of(k), s))
        pl.semaphore_wait(barrier, shards - 1)

        @pl.when(relays)
        def _():
            wait_for(relay, relay_recv)
            send(relay, first, relay_send, land_recv.at[0], (r, last))

        wait_for(held.at[pl.ds(0, regions - 1)], gather_recv)
        def spread(dst):
            for w in order:
                send(held.at[:, s ^ w], dst, land_send, land_recv.at[s], (r, s ^ w))
            pltpu.make_async_copy(held.at[:, s], dst, land_recv.at[s]).start()

        @pl.when(fed)
        def _():
            @pl.when(pair > 0)
            def _():
                send(held.at[:, last], first, land_send, land_recv.at[0], (r, last))

            for w in order[1:]:
                send(held.at[:, w], first, land_send, land_recv.at[0], (r, w))
            pltpu.make_async_copy(held.at[:, 0], first, land_recv.at[0]).start()

        @pl.when((s >= starts[1]) & (s < starts[2]))
        def _():
            spread(second.at[:, :, s - starts[1]])

        @pl.when(s >= starts[2])
        def _():
            spread(third.at[:, :, s - starts[2]])

        for copy in local:
            copy.wait()
        for a, b, _, sem in lists:
            wait_for(b, sem)
        for a, b, sem in weights:
            wait_for(b.at[0], sem)

        indices = ((near_0, region_0, block_0), (near_1, region_1, block_1))

        def residuals(half, ref, count):
            near_i, region_i, block_i = indices[half]
            here = r - 1 + half
            left = []
            for b in range(blocks):
                x = [ref[here, near_i[b, j]] for j in range(near)]
                x += [ref[region_i[j, b], block_i[j, b]] for j in range(far)]
                x = jnp.concatenate([v.reshape(count * rows, width) for v in x], axis=1)
                mean = jnp.dot(x, coef_w[half, b].reshape((near + far) * width, width),
                               preferred_element_type=jnp.float32)
                mine = ref[here, b].reshape(count * rows, width).astype(jnp.float32)
                left.append((mine - mean).astype(jnp.bfloat16))
            return left

        def give_back(half, left, start, count):
            here = r - 1 + half
            for b in range(blocks):
                white = jnp.dot(left[b], inv_w[half, b], preferred_element_type=jnp.float32)
                white = white.astype(jnp.bfloat16).reshape(count, rows, width)
                stage[half, pl.ds(start, count), b] = white
            for k in range(start, start + count):
                if half == 0:
                    send(stage.at[half, k], out.at[s], back_send, back_recv, (here, k))
                else:
                    @pl.when(s != k)
                    def _():
                        send(stage.at[half, k], out.at[s], back_send, back_recv, (here, k))

                    @pl.when(s == k)
                    def _():
                        pltpu.make_async_copy(stage.at[half, k], out.at[s], back_recv).start()

        def whiten(ref, start, count):
            for half in range(CORES):
                give_back(half, residuals(half, ref, count), start, count)

        part = held.at[:, 0]
        for ref, start, stop in zip((first, second, third), starts, starts[1:]):
            for k in range(start, stop):
                wait_for(part, land_recv.at[k])
            whiten(ref, start, stop - start)

        for k in range(1, chips):
            wait_for(held.at[r], gather_send.at[0])
        wait_for(held.at[:, pl.ds(0, shards - 2)], land_send)

        @pl.when((s > 0) | (pair > 0))
        def _():
            wait_for(part, land_send)

        @pl.when(fed)
        def _():
            wait_for(relay.at[0], relay_send)

        @pl.when(relays)
        def _():
            wait_for(relay, relay_send)

        wait_for(stage.at[0], back_send)
        wait_for(stage.at[1, pl.ds(0, shards - 1)], back_send)
        wait_for(out, back_recv)


def body(fields, near_coef, far_coef, inv_factor, near_block, far_region, far_block):
    shards, regions = lax.axis_size("shard"), lax.axis_size("region")
    rows, columns = fields.shape
    blocks, width = near_coef.shape[0], near_coef.shape[3]
    tiles = columns // width
    tiled = jnp.transpose(fields.reshape(rows, tiles, width), (1, 0, 2))
    tiled = tiled.reshape(shards, blocks, rows, width)
    hbm = pl.BlockSpec(memory_space=pl.ANY)
    half = jnp.bfloat16
    white = pl.pallas_call(
        functools.partial(kernel, regions, shards),
        out_shape=pltpu.VMEM(tiled.shape, half),
        in_specs=[hbm] * 7,
        out_specs=pl.BlockSpec(memory_space=pltpu.VMEM),
        scratch_shapes=[
            pltpu.VMEM((regions, shards, blocks, rows, width), half),
            pltpu.VMEM((regions, blocks, rows, width), half),
            pltpu.VMEM((regions, blocks, rows, width), half),
            pltpu.VMEM((regions, blocks, shards // 2 - 1, rows, width), half),
            pltpu.VMEM((regions, blocks, shards - shards // 2, rows, width), half),
            pltpu.VMEM((CORES, blocks, near_coef.shape[1] + far_coef.shape[1], width, width), half),
            pltpu.VMEM((CORES, *inv_factor.shape), half),
            pltpu.VMEM((CORES, shards, blocks, rows, width), half),
        ] + [pltpu.SMEM(a.shape, jnp.int32) for a in (near_block, far_region.T, far_block.T)] * 2 + [
            pltpu.SemaphoreType.DMA((7,)),
            pltpu.SemaphoreType.REGULAR,
            pltpu.SemaphoreType.DMA((1,)),
            pltpu.SemaphoreType.DMA,
            pltpu.SemaphoreType.DMA((1,)),
            pltpu.SemaphoreType.DMA((6,)),
            pltpu.SemaphoreType.DMA,
            pltpu.SemaphoreType.DMA((shards,)),
            pltpu.SemaphoreType.DMA,
            pltpu.SemaphoreType.DMA,
            pltpu.SemaphoreType.DMA,
            pltpu.SemaphoreType.DMA,
        ],
        compiler_params=pltpu.CompilerParams(collective_id=0, has_side_effects=True),
    )(tiled, near_coef, far_coef, inv_factor, near_block, far_region.T, far_block.T)
    white = white.reshape(tiles, rows, width)
    return jnp.transpose(white, (1, 0, 2)).reshape(rows, columns)


def solution(mesh):
    return jax.shard_map(
        body,
        mesh=mesh,
        in_specs=(
            P("shard", "region"),
            P(("region", "shard"), None, None, None),
            P(("region", "shard"), None, None, None),
            P(("region", "shard"), None, None),
            P(("region", "shard"), None),
            P(("region", "shard"), None),
            P(("region", "shard"), None),
        ),
        out_specs=P("shard", "region"),
        check_vma=False,
    )
```

```python
import functools

import jax
import jax.numpy as jnp
from jax import lax
from jax.experimental import pallas as pl
from jax.experimental.pallas import tpu as pltpu
from jax.sharding import PartitionSpec as P

CORES = 2
RELAY = 1
MESH = pl.DeviceIdType.MESH


def kernel(regions, shards, fields, near_coef, far_coef, inv_factor, near_list,
           region_list, block_list, out, held, relay, early, first, second, middle, third, coef_w, inv_w, stage,
           near_0, region_0, block_0, near_1, region_1, block_1,
           load_sem, ready, gather_send, gather_recv, weight_send, weight_recv,
           land_send, land_recv, back_send, back_recv, relay_send, relay_recv, early_recv):
    blocks, rows, width = held.shape[2:]
    near, far = near_coef.shape[1], far_coef.shape[1]
    members = shards * rows
    chips = regions // CORES
    r, s = lax.axis_index("region"), lax.axis_index("shard")
    core = lax.rem(r, CORES)
    pair = lax.div(r, CORES)
    lead, mate = core == CORES - 1, core == 0
    order = list(reversed(range(1, shards)))
    last = shards - 1
    starts = (0, 1, 2, shards // 2, shards)
    relays, fed = (s == RELAY) & (pair == 0), s == 0
    farthest = (s == last) & (pair == 0)
    close, remote = pl.ds(0, CORES), pl.ds(CORES, regions - CORES)
    via = (CORES - 1, RELAY)

    def odd_of(k):
        return lax.rem(pair + k, chips) * CORES + CORES - 1

    def wait_for(ref, sem):
        pltpu.make_async_copy(ref, ref, sem).wait()

    def send(src, dst, send_sem, recv_sem, to):
        pltpu.make_async_remote_copy(
            src_ref=src, dst_ref=dst, send_sem=send_sem, recv_sem=recv_sem,
            device_id=to, device_id_type=MESH).start()

    barrier = pltpu.get_barrier_semaphore()
    load = pltpu.make_async_copy(fields, held.at[r], load_sem.at[0])
    weights = [(near_coef, coef_w.at[:, :, pl.ds(0, near)], weight_recv.at[0]),
               (far_coef, coef_w.at[:, :, pl.ds(near, far)], weight_recv.at[1]),
               (inv_factor, inv_w, weight_recv.at[2])]
    lists = [(near_list, near_0, near_1, weight_recv.at[3]),
             (region_list, region_0, region_1, weight_recv.at[4]),
             (block_list, block_0, block_1, weight_recv.at[5])]
    local = [pltpu.make_async_copy(a, b.at[1], load_sem.at[1 + i])
             for i, (a, b, _) in enumerate(weights)]
    local += [pltpu.make_async_copy(a, b, load_sem.at[4 + i])
              for i, (a, _, b, _) in enumerate(lists)]

    def greet(to):
        pl.semaphore_signal(barrier, inc=1, device_id=to, device_id_type=MESH)

    @pl.when(lead)
    def _():
        @pl.when(relays)
        def _():
            for k in reversed(range(chips)):
                greet((k * CORES, 0))

        for w in order:
            greet((r, s ^ w))
        for k in range(chips):
            greet((lax.rem(pair + k, chips) * CORES, s))
        load.start()

    @pl.when(mate & fed)
    def _():
        load.start()
        pl.semaphore_wait(barrier, chips + 1)
        load.wait()
        send(held.at[r, last], relay.at[r], relay_send, relay_recv.at[jnp.minimum(pair, 1)], via)
        pl.semaphore_signal(ready, inc=1, device_id=(r + 1, s), device_id_type=MESH)
        for k in reversed(range(chips)):
            send(held.at[r], held.at[r], gather_send.at[0], gather_recv, (odd_of(k), s))


    @pl.when(mate & (s > 0))
    def _():
        pl.semaphore_wait(barrier, chips)
        for k in reversed(range(chips)):
            send(fields, held.at[r], gather_send.at[0], gather_recv, (odd_of(k), s))
        pl.semaphore_signal(ready, inc=1, device_id=(r + 1, s), device_id_type=MESH)

    @pl.when(mate)
    def _():
        mine = (r + 1, s)
        for a, b, _, sem in lists:
            send(a, b, weight_send.at[0], sem, mine)
        for a, b, sem in weights:
            send(a, b.at[0], weight_send.at[0], sem, mine)
        for k in range(chips):
            wait_for(held.at[r], gather_send.at[0])
        for a, b, _, sem in lists:
            wait_for(a, weight_send.at[0])
        for a, b, sem in weights:
            wait_for(a, weight_send.at[0])

        @pl.when(fed)
        def _():
            wait_for(relay.at[0], relay_send)

        wait_for(out, back_recv)

    @pl.when(lead)
    def _():
        for copy in local:
            copy.start()
        load.wait()
        pl.semaphore_wait(ready, 1)

        @pl.when(fed)
        def _():
            send(held.at[r, last], relay.at[r], relay_send, relay_recv.at[jnp.minimum(pair, 1)], via)

        for k in range(1, chips):
            send(held.at[r], held.at[r], gather_send.at[0], gather_recv, (odd_of(k), s))
        pl.semaphore_wait(barrier, shards - 1)

        @pl.when(relays)
        def _():
            wait_for(relay.at[close], relay_recv.at[0])
            send(relay.at[close], early, relay_send, early_recv, (r, last))
            wait_for(relay.at[remote], relay_recv.at[1])
            send(relay.at[remote], first.at[remote], relay_send, land_recv.at[0], (r, last))

        wait_for(held.at[pl.ds(0, regions - 1)], gather_recv)
        def spread(dst):
            for w in order:
                send(held.at[:, s ^ w], dst, land_send, land_recv.at[s], (r, s ^ w))
            pltpu.make_async_copy(held.at[:, s], dst, land_recv.at[s]).start()

        @pl.when(fed)
        def _():
            @pl.when(pair > 0)
            def _():
                send(held.at[:, last], first, land_send, land_recv.at[0], (r, last))

            for w in order[1:]:
                send(held.at[:, w], first, land_send, land_recv.at[0], (r, w))
            pltpu.make_async_copy(held.at[:, 0], first, land_recv.at[0]).start()

        @pl.when((s >= starts[1]) & (s < starts[2]))
        def _():
            spread(second.at[:, :, s - starts[1]])

        @pl.when((s >= starts[2]) & (s < starts[3]))
        def _():
            spread(middle.at[:, :, s - starts[2]])

        @pl.when(s >= starts[3])
        def _():
            spread(third.at[:, :, s - starts[3]])

        for copy in local:
            copy.wait()
        for a, b, _, sem in lists:
            wait_for(b, sem)
        for a, b, sem in weights:
            wait_for(b.at[0], sem)

        indices = [([[near_i[b, j] for j in range(near)] for b in range(blocks)],
                    [[(region_i[j, b], block_i[j, b]) for j in range(far)] for b in range(blocks)])
                   for near_i, region_i, block_i in ((near_0, region_0, block_0),
                                                     (near_1, region_1, block_1))]

        def rows_of(ref, picks, m):
            return jnp.concatenate([ref[k].reshape(m, width) for k in picks], axis=1)

        def weighted(x, half, b, at, count):
            w = coef_w[half, b, at:at + count].reshape(count * width, width)
            return jnp.dot(x, w, preferred_element_type=jnp.float32)

        def residuals(half, ref, count):
            near_at, far_at = indices[half]
            here = r - 1 + half
            m = count * rows
            left = []
            for b in range(blocks):
                x = rows_of(ref, [(here, k) for k in near_at[b]] + far_at[b], m)
                mean = weighted(x, half, b, 0, near + far)
                mine = ref[here, b].reshape(m, width).astype(jnp.float32)
                left.append((mine - mean).astype(jnp.bfloat16))
            return left

        def without_near(half):
            left = []
            for b in range(blocks):
                x = rows_of(early, [(half, k) for k in indices[half][0][b]], rows)
                left.append(early[half, b].astype(jnp.float32) - weighted(x, half, b, 0, near))
            return left

        def without_far(half, left):
            return [(left[b] - weighted(rows_of(first, indices[half][1][b], rows), half, b, near, far)
                     ).astype(jnp.bfloat16) for b in range(blocks)]

        def give_back(half, left, start, count):
            here = r - 1 + half
            m = count * rows
            for b in range(0, blocks, 2):
                x, y = left[b], left[b + 1]
                top = jnp.concatenate([x, jnp.zeros_like(x)], axis=1)
                both = jnp.concatenate([top, jnp.concatenate([jnp.zeros_like(y), y], axis=1)], axis=0)
                white = jnp.dot(both, inv_w[half, b:b + 2].reshape(2 * width, width),
                                preferred_element_type=jnp.float32)
                white = white.astype(jnp.bfloat16)
                stage[half, pl.ds(start, count), b] = white[:m].reshape(count, rows, width)
                stage[half, pl.ds(start, count), b + 1] = white[m:].reshape(count, rows, width)
            for k in range(start, start + count):
                if half == 0:
                    send(stage.at[half, k], out.at[s], back_send, back_recv, (here, k))
                else:
                    @pl.when(s != k)
                    def _():
                        send(stage.at[half, k], out.at[s], back_send, back_recv, (here, k))

                    @pl.when(s == k)
                    def _():
                        pltpu.make_async_copy(stage.at[half, k], out.at[s], back_recv).start()

        def whiten(ref, start, count):
            for half in range(CORES):
                give_back(half, residuals(half, ref, count), start, count)

        part = held.at[:, 0]
        @pl.when(farthest)
        def _():
            wait_for(early, early_recv)
            first[close] = early[...]
            left = [without_near(half) for half in range(CORES)]
            wait_for(first.at[remote], land_recv.at[0])
            for half in range(CORES):
                give_back(half, without_far(half, left[half]), 0, 1)

        @pl.when(jnp.logical_not(farthest))
        def _():
            wait_for(part, land_recv.at[0])
            whiten(first, 0, 1)

        for ref, start, stop in zip((second, middle, third), starts[1:], starts[2:]):
            for k in range(start, stop):
                wait_for(part, land_recv.at[k])
            whiten(ref, start, stop - start)

        for k in range(1, chips):
            wait_for(held.at[r], gather_send.at[0])
        wait_for(held.at[:, pl.ds(0, shards - 2)], land_send)

        @pl.when((s > 0) | (pair > 0))
        def _():
            wait_for(part, land_send)

        @pl.when(fed)
        def _():
            wait_for(relay.at[0], relay_send)

        @pl.when(relays)
        def _():
            wait_for(relay, relay_send)

        wait_for(stage.at[0], back_send)
        wait_for(stage.at[1, pl.ds(0, shards - 1)], back_send)
        wait_for(out, back_recv)


def body(fields, near_coef, far_coef, inv_factor, near_block, far_region, far_block):
    shards, regions = lax.axis_size("shard"), lax.axis_size("region")
    rows, columns = fields.shape
    blocks, width = near_coef.shape[0], near_coef.shape[3]
    tiles = columns // width
    tiled = jnp.transpose(fields.reshape(rows, tiles, width), (1, 0, 2))
    tiled = tiled.reshape(shards, blocks, rows, width)
    hbm = pl.BlockSpec(memory_space=pl.ANY)
    half = jnp.bfloat16
    white = pl.pallas_call(
        functools.partial(kernel, regions, shards),
        out_shape=pltpu.VMEM(tiled.shape, half),
        in_specs=[hbm] * 7,
        out_specs=pl.BlockSpec(memory_space=pltpu.VMEM),
        scratch_shapes=[
            pltpu.VMEM((regions, shards, blocks, rows, width), half),
            pltpu.VMEM((regions, blocks, rows, width), half),
            pltpu.VMEM((CORES, blocks, rows, width), half),
            pltpu.VMEM((regions, blocks, rows, width), half),
            pltpu.VMEM((regions, blocks, 1, rows, width), half),
            pltpu.VMEM((regions, blocks, shards // 2 - 2, rows, width), half),
            pltpu.VMEM((regions, blocks, shards - shards // 2, rows, width), half),
            pltpu.VMEM((CORES, blocks, near_coef.shape[1] + far_coef.shape[1], width, width), half),
            pltpu.VMEM((CORES, *inv_factor.shape), half),
            pltpu.VMEM((CORES, shards, blocks, rows, width), half),
        ] + [pltpu.SMEM(a.shape, jnp.int32) for a in (near_block, far_region.T, far_block.T)] * 2 + [
            pltpu.SemaphoreType.DMA((7,)),
            pltpu.SemaphoreType.REGULAR,
            pltpu.SemaphoreType.DMA((1,)),
            pltpu.SemaphoreType.DMA,
            pltpu.SemaphoreType.DMA((1,)),
            pltpu.SemaphoreType.DMA((6,)),
            pltpu.SemaphoreType.DMA,
            pltpu.SemaphoreType.DMA((shards,)),
            pltpu.SemaphoreType.DMA,
            pltpu.SemaphoreType.DMA,
            pltpu.SemaphoreType.DMA,
            pltpu.SemaphoreType.DMA((2,)),
            pltpu.SemaphoreType.DMA,
        ],
        compiler_params=pltpu.CompilerParams(collective_id=0, has_side_effects=True),
    )(tiled, near_coef, far_coef, inv_factor, near_block, far_region.T, far_block.T)
    white = white.reshape(tiles, rows, width)
    return jnp.transpose(white, (1, 0, 2)).reshape(rows, columns)


def solution(mesh):
    return jax.shard_map(
        body,
        mesh=mesh,
        in_specs=(
            P("shard", "region"),
            P(("region", "shard"), None, None, None),
            P(("region", "shard"), None, None, None),
            P(("region", "shard"), None, None),
            P(("region", "shard"), None),
            P(("region", "shard"), None),
            P(("region", "shard"), None),
        ),
        out_specs=P("shard", "region"),
        check_vma=False,
    )
```

```python
import functools

import jax
import jax.numpy as jnp
from jax import lax
from jax.experimental import pallas as pl
from jax.experimental.pallas import tpu as pltpu
from jax.sharding import PartitionSpec as P

CORES = 2
RELAY = 1
MESH = pl.DeviceIdType.MESH


def kernel(regions, shards, fields, near_coef, far_coef, inv_factor, near_list,
           region_list, block_list, out, held, relay, early, first, second, middle, third,
           weight, stage, near_of, region_of, block_of, ready, list_sem, weight_sem,
           send_sem, gather_sem, land_sem, back_sem, relay_sem):
    blocks, rows, width = held.shape[2:]
    near, far = near_coef.shape[1], far_coef.shape[1]
    members = shards * rows
    chips = regions // CORES
    r, s = lax.axis_index("region"), lax.axis_index("shard")
    core = lax.rem(r, CORES)
    pair = lax.div(r, CORES)
    lead, mate = core == CORES - 1, core == 0
    order = list(reversed(range(1, shards)))
    last = shards - 1
    starts = (0, 1, 2, shards // 2, shards)
    relays, fed = (s == RELAY) & (pair == 0), s == 0
    farthest = (s == last) & (pair == 0)
    close, remote = pl.ds(0, CORES), pl.ds(CORES, regions - CORES)
    via = (CORES - 1, RELAY)

    def odd_of(k):
        return lax.rem(pair + k, chips) * CORES + CORES - 1

    def wait_for(ref, sem):
        pltpu.make_async_copy(ref, ref, sem).wait()

    def send(src, dst, sem, to):
        pltpu.make_async_remote_copy(
            src_ref=src, dst_ref=dst, send_sem=send_sem, recv_sem=sem,
            device_id=to, device_id_type=MESH).start()

    barrier = pltpu.get_barrier_semaphore()
    load = pltpu.make_async_copy(fields, held.at[r], back_sem)

    def parts(half):
        return [(near_list, near_of.at[half], list_sem.at[0]),
                (region_list, region_of.at[half], list_sem.at[1]),
                (block_list, block_of.at[half], list_sem.at[2]),
                (near_coef, weight.at[half, :, pl.ds(0, near)], weight_sem),
                (far_coef, weight.at[half, :, pl.ds(near, far)], weight_sem),
                (inv_factor, weight.at[half, :, near + far], weight_sem)]

    def greet(to):
        pl.semaphore_signal(barrier, inc=1, device_id=to, device_id_type=MESH)

    @pl.when(lead)
    def _():
        @pl.when(relays)
        def _():
            for k in reversed(range(chips)):
                greet((k * CORES, 0))

        for w in order:
            greet((r, s ^ w))
        for k in range(chips):
            greet((lax.rem(pair + k, chips) * CORES, s))
        load.start()

    @pl.when(mate & fed)
    def _():
        load.start()
        pl.semaphore_wait(barrier, chips + 1)
        load.wait()
        send(held.at[r, last], relay.at[r], relay_sem.at[jnp.minimum(pair, 1)], via)
        pl.semaphore_signal(ready, inc=1, device_id=(r + 1, s), device_id_type=MESH)
        for k in reversed(range(chips)):
            send(held.at[r], held.at[r], gather_sem, (odd_of(k), s))


    @pl.when(mate & (s > 0))
    def _():
        pl.semaphore_wait(barrier, chips)
        for k in reversed(range(chips)):
            send(fields, held.at[r], gather_sem, (odd_of(k), s))
        pl.semaphore_signal(ready, inc=1, device_id=(r + 1, s), device_id_type=MESH)

    @pl.when(mate)
    def _():
        for a, b, sem in parts(0):
            send(a, b, sem, (r + 1, s))
        for k in range(chips):
            wait_for(held.at[r], send_sem)
        for a, _, _ in parts(0):
            wait_for(a, send_sem)

        @pl.when(fed)
        def _():
            wait_for(relay.at[0], send_sem)

        wait_for(out, back_sem)

    @pl.when(lead)
    def _():
        for a, b, sem in parts(1):
            pltpu.make_async_copy(a, b, sem).start()
        load.wait()
        pl.semaphore_wait(ready, 1)

        @pl.when(fed)
        def _():
            send(held.at[r, last], relay.at[r], relay_sem.at[jnp.minimum(pair, 1)], via)

        for k in range(1, chips):
            send(held.at[r], held.at[r], gather_sem, (odd_of(k), s))
        pl.semaphore_wait(barrier, shards - 1)

        @pl.when(relays)
        def _():
            wait_for(relay.at[close], relay_sem.at[0])
            send(relay.at[close], early, relay_sem.at[0], (r, last))
            wait_for(relay.at[remote], relay_sem.at[1])
            send(relay.at[remote], first.at[remote], land_sem.at[0], (r, last))

        wait_for(held.at[pl.ds(0, regions - 1)], gather_sem)
        def spread(dst, sem):
            for w in order:
                send(held.at[:, s ^ w], dst, sem, (r, s ^ w))
            pltpu.make_async_copy(held.at[:, s], dst, sem).start()

        @pl.when(fed)
        def _():
            @pl.when(pair > 0)
            def _():
                send(held.at[:, last], first, land_sem.at[0], (r, last))

            for w in order[1:]:
                send(held.at[:, w], first, land_sem.at[0], (r, w))
            pltpu.make_async_copy(held.at[:, 0], first, land_sem.at[0]).start()

        batches = (first, second, middle, third)
        for i in range(1, len(batches)):
            @pl.when((s >= starts[i]) & (s < starts[i + 1]))
            def _():
                spread(batches[i].at[:, :, s - starts[i]], land_sem.at[i])

        for ref, sem in ((near_of, list_sem.at[0]), (region_of, list_sem.at[1]),
                         (block_of, list_sem.at[2]), (weight, weight_sem)):
            wait_for(ref, sem)

        indices = [([[near_of[half, b, j] for j in range(near)] for b in range(blocks)],
                    [[(region_of[half, j, b], block_of[half, j, b]) for j in range(far)]
                     for b in range(blocks)])
                   for half in range(CORES)]

        def rows_of(ref, picks, m):
            return jnp.concatenate([ref[k].reshape(m, width) for k in picks], axis=1)

        def weighted(x, half, b, at, count):
            w = weight[half, b, at:at + count].reshape(count * width, width)
            return jnp.dot(x, w, preferred_element_type=jnp.float32)

        def residuals(half, ref, count):
            near_at, far_at = indices[half]
            here = r - 1 + half
            m = count * rows
            left = []
            for b in range(blocks):
                x = rows_of(ref, [(here, k) for k in near_at[b]] + far_at[b], m)
                mean = weighted(x, half, b, 0, near + far)
                mine = ref[here, b].reshape(m, width).astype(jnp.float32)
                left.append((mine - mean).astype(jnp.bfloat16))
            return left

        def without_near(half):
            left = []
            for b in range(blocks):
                x = rows_of(early, [(half, k) for k in indices[half][0][b]], rows)
                left.append(early[half, b].astype(jnp.float32) - weighted(x, half, b, 0, near))
            return left

        def without_far(half, left):
            return [(left[b] - weighted(rows_of(first, indices[half][1][b], rows), half, b, near, far)
                     ).astype(jnp.bfloat16) for b in range(blocks)]

        def give_back(half, left, start, count):
            here = r - 1 + half
            m = count * rows
            for b in range(0, blocks, 2):
                x, y = left[b], left[b + 1]
                top = jnp.concatenate([x, jnp.zeros_like(x)], axis=1)
                both = jnp.concatenate([top, jnp.concatenate([jnp.zeros_like(y), y], axis=1)], axis=0)
                white = jnp.dot(both, weight[half, b:b + 2, near + far].reshape(2 * width, width),
                                preferred_element_type=jnp.float32)
                white = white.astype(jnp.bfloat16)
                stage[half, pl.ds(start, count), b] = white[:m].reshape(count, rows, width)
                stage[half, pl.ds(start, count), b + 1] = white[m:].reshape(count, rows, width)
            for k in range(start, start + count):
                if half == 0:
                    send(stage.at[half, k], out.at[s], back_sem, (here, k))
                else:
                    @pl.when(s != k)
                    def _():
                        send(stage.at[half, k], out.at[s], back_sem, (here, k))

                    @pl.when(s == k)
                    def _():
                        pltpu.make_async_copy(stage.at[half, k], out.at[s], back_sem).start()

        def whiten(ref, start, count):
            for half in range(CORES):
                give_back(half, residuals(half, ref, count), start, count)

        @pl.when(farthest)
        def _():
            wait_for(early, relay_sem.at[0])
            first[close] = early[...]
            left = [without_near(half) for half in range(CORES)]
            wait_for(first.at[remote], land_sem.at[0])
            for half in range(CORES):
                give_back(half, without_far(half, left[half]), 0, 1)

        @pl.when(jnp.logical_not(farthest))
        def _():
            wait_for(first, land_sem.at[0])
            whiten(first, 0, 1)

        for i in range(1, len(batches)):
            wait_for(batches[i], land_sem.at[i])
            whiten(batches[i], starts[i], starts[i + 1] - starts[i])

        for k in range(1, chips):
            wait_for(held.at[r], send_sem)
        wait_for(held.at[:, pl.ds(0, shards - 2)], send_sem)

        @pl.when((s > 0) | (pair > 0))
        def _():
            wait_for(held.at[:, 0], send_sem)

        @pl.when(fed)
        def _():
            wait_for(relay.at[0], send_sem)

        @pl.when(relays)
        def _():
            wait_for(relay, send_sem)

        wait_for(stage.at[0], send_sem)
        wait_for(stage.at[1, pl.ds(0, shards - 1)], send_sem)
        wait_for(out, back_sem)


def body(fields, near_coef, far_coef, inv_factor, near_block, far_region, far_block):
    shards, regions = lax.axis_size("shard"), lax.axis_size("region")
    rows, columns = fields.shape
    blocks, width = near_coef.shape[0], near_coef.shape[3]
    tiles = columns // width
    tiled = jnp.transpose(fields.reshape(rows, tiles, width), (1, 0, 2))
    tiled = tiled.reshape(shards, blocks, rows, width)
    hbm = pl.BlockSpec(memory_space=pl.ANY)
    half = jnp.bfloat16
    white = pl.pallas_call(
        functools.partial(kernel, regions, shards),
        out_shape=pltpu.VMEM(tiled.shape, half),
        in_specs=[hbm] * 7,
        out_specs=pl.BlockSpec(memory_space=pltpu.VMEM),
        scratch_shapes=[
            pltpu.VMEM((regions, shards, blocks, rows, width), half),
            pltpu.VMEM((regions, blocks, rows, width), half),
            pltpu.VMEM((CORES, blocks, rows, width), half),
            pltpu.VMEM((regions, blocks, rows, width), half),
            pltpu.VMEM((regions, blocks, 1, rows, width), half),
            pltpu.VMEM((regions, blocks, shards // 2 - 2, rows, width), half),
            pltpu.VMEM((regions, blocks, shards - shards // 2, rows, width), half),
            pltpu.VMEM((CORES, blocks, near_coef.shape[1] + far_coef.shape[1] + 1, width, width), half),
            pltpu.VMEM((CORES, shards, blocks, rows, width), half),
            pltpu.SMEM((CORES, *near_block.shape), jnp.int32),
            pltpu.SMEM((CORES, *far_region.T.shape), jnp.int32),
            pltpu.SMEM((CORES, *far_block.T.shape), jnp.int32),
            pltpu.SemaphoreType.REGULAR,
            pltpu.SemaphoreType.DMA((3,)),
            pltpu.SemaphoreType.DMA,
            pltpu.SemaphoreType.DMA,
            pltpu.SemaphoreType.DMA,
            pltpu.SemaphoreType.DMA((4,)),
            pltpu.SemaphoreType.DMA,
            pltpu.SemaphoreType.DMA((2,)),
        ],
        compiler_params=pltpu.CompilerParams(collective_id=0, has_side_effects=True),
    )(tiled, near_coef, far_coef, inv_factor, near_block, far_region.T, far_block.T)
    white = white.reshape(tiles, rows, width)
    return jnp.transpose(white, (1, 0, 2)).reshape(rows, columns)


def solution(mesh):
    return jax.shard_map(
        body,
        mesh=mesh,
        in_specs=(
            P("shard", "region"),
            P(("region", "shard"), None, None, None),
            P(("region", "shard"), None, None, None),
            P(("region", "shard"), None, None),
            P(("region", "shard"), None),
            P(("region", "shard"), None),
            P(("region", "shard"), None),
        ),
        out_specs=P("shard", "region"),
        check_vma=False,
    )
```

```python
import functools

import jax
import jax.numpy as jnp
from jax import lax
from jax.experimental import pallas as pl
from jax.experimental.pallas import tpu as pltpu
from jax.sharding import PartitionSpec as P

CORES = 2
RELAY = 1
MESH = pl.DeviceIdType.MESH


def kernel(regions, shards, fields, near_coef, far_coef, inv_factor, near_list,
           region_list, block_list, out, held, relay, early, first, second, middle, third,
           weight, stage, near_of, far_of, ready, list_sem, weight_sem,
           send_sem, gather_sem, land_sem, back_sem, relay_sem):
    blocks, rows, width = held.shape[2:]
    near, far = near_coef.shape[1], far_coef.shape[1]
    members = shards * rows
    chips = regions // CORES
    r, s = lax.axis_index("region"), lax.axis_index("shard")
    core = lax.rem(r, CORES)
    pair = lax.div(r, CORES)
    lead, mate = core == CORES - 1, core == 0
    order = list(reversed(range(1, shards)))
    last = shards - 1
    starts = (0, 1, 2, shards // 2, shards)
    relays, fed = (s == RELAY) & (pair == 0), s == 0
    farthest = (s == last) & (pair == 0)
    close, remote = pl.ds(0, CORES), pl.ds(CORES, regions - CORES)
    via = (CORES - 1, RELAY)

    def odd_of(k):
        return lax.rem(pair + k, chips) * CORES + CORES - 1

    def wait_for(ref, sem):
        pltpu.make_async_copy(ref, ref, sem).wait()

    def send(src, dst, sem, to):
        pltpu.make_async_remote_copy(
            src_ref=src, dst_ref=dst, send_sem=send_sem, recv_sem=sem,
            device_id=to, device_id_type=MESH).start()

    barrier = pltpu.get_barrier_semaphore()
    load = pltpu.make_async_copy(fields, held.at[r], back_sem)

    def parts(half):
        return [(near_list, near_of.at[half], list_sem.at[0]),
                (region_list, far_of.at[half, 0], list_sem.at[1]),
                (block_list, far_of.at[half, 1], list_sem.at[1]),
                (near_coef, weight.at[half, :, pl.ds(0, near)], weight_sem),
                (far_coef, weight.at[half, :, pl.ds(near, far)], weight_sem),
                (inv_factor, weight.at[half, :, near + far], weight_sem)]

    def greet(to):
        pl.semaphore_signal(barrier, inc=1, device_id=to, device_id_type=MESH)

    @pl.when(lead)
    def _():
        @pl.when(relays)
        def _():
            for k in reversed(range(chips)):
                greet((k * CORES, 0))

        for w in order:
            greet((r, s ^ w))
        for k in range(chips):
            greet((lax.rem(pair + k, chips) * CORES, s))
        load.start()

    @pl.when(mate & fed)
    def _():
        load.start()
        pl.semaphore_wait(barrier, chips + 1)
        pl.semaphore_signal(ready, inc=1, device_id=(r + 1, s), device_id_type=MESH)
        load.wait()
        send(held.at[r, last], relay.at[r], relay_sem.at[jnp.minimum(pair, 1)], via)
        for k in reversed(range(chips)):
            send(held.at[r], held.at[r], gather_sem, (odd_of(k), s))


    @pl.when(mate & (s > 0))
    def _():
        pl.semaphore_wait(barrier, chips)
        for k in reversed(range(chips)):
            send(fields, held.at[r], gather_sem, (odd_of(k), s))
        pl.semaphore_signal(ready, inc=1, device_id=(r + 1, s), device_id_type=MESH)

    @pl.when(mate)
    def _():
        for a, b, sem in parts(0):
            send(a, b, sem, (r + 1, s))
        for k in range(chips):
            wait_for(held.at[r], send_sem)
        for a, _, _ in parts(0):
            wait_for(a, send_sem)

        @pl.when(fed)
        def _():
            wait_for(relay.at[0], send_sem)

        wait_for(out, back_sem)

    @pl.when(lead)
    def _():
        for a, b, sem in parts(1):
            pltpu.make_async_copy(a, b, sem).start()
        load.wait()
        pl.semaphore_wait(ready, 1)

        @pl.when(fed)
        def _():
            send(held.at[r, last], relay.at[r], relay_sem.at[jnp.minimum(pair, 1)], via)

        for k in range(1, chips):
            send(held.at[r], held.at[r], gather_sem, (odd_of(k), s))
        pl.semaphore_wait(barrier, shards - 1)

        @pl.when(relays)
        def _():
            wait_for(relay.at[close], relay_sem.at[0])
            send(relay.at[close], early, relay_sem.at[0], (r, last))
            wait_for(relay.at[remote], relay_sem.at[1])
            send(relay.at[remote], first.at[remote], land_sem.at[0], (r, last))

        wait_for(held.at[pl.ds(0, regions - 1)], gather_sem)
        def spread(dst, sem):
            for w in order:
                send(held.at[:, s ^ w], dst, sem, (r, s ^ w))
            pltpu.make_async_copy(held.at[:, s], dst, sem).start()

        @pl.when(fed)
        def _():
            @pl.when(pair > 0)
            def _():
                send(held.at[:, last], first, land_sem.at[0], (r, last))

            for w in [last - 2, last - 1, *order[3:]]:
                send(held.at[:, w], first, land_sem.at[0], (r, w))
            pltpu.make_async_copy(held.at[:, 0], first, land_sem.at[0]).start()

        batches = (first, second, middle, third)
        for i in range(1, len(batches)):
            @pl.when((s >= starts[i]) & (s < starts[i + 1]))
            def _():
                spread(batches[i].at[:, :, s - starts[i]], land_sem.at[i])

        for ref, sem in ((near_of, list_sem.at[0]), (far_of, list_sem.at[1]), (weight, weight_sem)):
            wait_for(ref, sem)

        indices = [([[near_of[half, b, j] for j in range(near)] for b in range(blocks)],
                    [[(far_of[half, 0, j, b], far_of[half, 1, j, b]) for j in range(far)]
                     for b in range(blocks)])
                   for half in range(CORES)]

        def rows_of(ref, picks, m):
            return jnp.concatenate([ref[k].reshape(m, width) for k in picks], axis=1)

        def weighted(x, half, b, at, count):
            w = weight[half, b, at:at + count].reshape(count * width, width)
            return jnp.dot(x, w, preferred_element_type=jnp.float32)

        def residuals(half, ref, count):
            near_at, far_at = indices[half]
            here = r - 1 + half
            m = count * rows
            left = []
            for b in range(blocks):
                x = rows_of(ref, [(here, k) for k in near_at[b]] + far_at[b], m)
                mean = weighted(x, half, b, 0, near + far)
                mine = ref[here, b].reshape(m, width).astype(jnp.float32)
                left.append((mine - mean).astype(jnp.bfloat16))
            return left

        def without_near(half):
            left = []
            for b in range(blocks):
                x = rows_of(early, [(half, k) for k in indices[half][0][b]], rows)
                left.append(early[half, b].astype(jnp.float32) - weighted(x, half, b, 0, near))
            return left

        def without_far(half, left):
            return [(left[b] - weighted(rows_of(first, indices[half][1][b], rows), half, b, near, far)
                     ).astype(jnp.bfloat16) for b in range(blocks)]

        def give_back(half, left, start, count):
            here = r - 1 + half
            m = count * rows
            for b in range(0, blocks, 2):
                x, y = left[b], left[b + 1]
                top = jnp.concatenate([x, jnp.zeros_like(x)], axis=1)
                both = jnp.concatenate([top, jnp.concatenate([jnp.zeros_like(y), y], axis=1)], axis=0)
                white = jnp.dot(both, weight[half, b:b + 2, near + far].reshape(2 * width, width),
                                preferred_element_type=jnp.float32)
                white = white.astype(jnp.bfloat16)
                stage[half, pl.ds(start, count), b] = white[:m].reshape(count, rows, width)
                stage[half, pl.ds(start, count), b + 1] = white[m:].reshape(count, rows, width)
            for k in range(start, start + count):
                if half == 0:
                    send(stage.at[half, k], out.at[s], back_sem, (here, k))
                else:
                    @pl.when(s != k)
                    def _():
                        send(stage.at[half, k], out.at[s], back_sem, (here, k))

                    @pl.when(s == k)
                    def _():
                        pltpu.make_async_copy(stage.at[half, k], out.at[s], back_sem).start()

        def whiten(ref, start, count):
            for half in range(CORES):
                give_back(half, residuals(half, ref, count), start, count)

        @pl.when(farthest)
        def _():
            wait_for(early, relay_sem.at[0])
            first[close] = early[...]
            left = [without_near(half) for half in range(CORES)]
            wait_for(first.at[remote], land_sem.at[0])
            for half in range(CORES):
                give_back(half, without_far(half, left[half]), 0, 1)

        @pl.when(jnp.logical_not(farthest))
        def _():
            wait_for(first, land_sem.at[0])
            whiten(first, 0, 1)

        for i in range(1, len(batches)):
            wait_for(batches[i], land_sem.at[i])
            whiten(batches[i], starts[i], starts[i + 1] - starts[i])

        for k in range(1, chips):
            wait_for(held.at[r], send_sem)
        wait_for(held.at[:, pl.ds(0, shards - 2)], send_sem)

        @pl.when((s > 0) | (pair > 0))
        def _():
            wait_for(held.at[:, 0], send_sem)

        @pl.when(fed)
        def _():
            wait_for(relay.at[0], send_sem)

        @pl.when(relays)
        def _():
            wait_for(relay, send_sem)

        wait_for(stage.at[0], send_sem)
        wait_for(stage.at[1, pl.ds(0, shards - 1)], send_sem)
        wait_for(out, back_sem)


def body(fields, near_coef, far_coef, inv_factor, near_block, far_region, far_block):
    shards, regions = lax.axis_size("shard"), lax.axis_size("region")
    rows, columns = fields.shape
    blocks, width = near_coef.shape[0], near_coef.shape[3]
    tiles = columns // width
    tiled = jnp.transpose(fields.reshape(rows, tiles, width), (1, 0, 2))
    tiled = tiled.reshape(shards, blocks, rows, width)
    hbm = pl.BlockSpec(memory_space=pl.ANY)
    half = jnp.bfloat16
    white = pl.pallas_call(
        functools.partial(kernel, regions, shards),
        out_shape=pltpu.VMEM(tiled.shape, half),
        in_specs=[hbm] * 7,
        out_specs=pl.BlockSpec(memory_space=pltpu.VMEM),
        scratch_shapes=[
            pltpu.VMEM((regions, shards, blocks, rows, width), half),
            pltpu.VMEM((regions, blocks, rows, width), half),
            pltpu.VMEM((CORES, blocks, rows, width), half),
            pltpu.VMEM((regions, blocks, rows, width), half),
            pltpu.VMEM((regions, blocks, 1, rows, width), half),
            pltpu.VMEM((regions, blocks, shards // 2 - 2, rows, width), half),
            pltpu.VMEM((regions, blocks, shards - shards // 2, rows, width), half),
            pltpu.VMEM((CORES, blocks, near_coef.shape[1] + far_coef.shape[1] + 1, width, width), half),
            pltpu.VMEM((CORES, shards, blocks, rows, width), half),
            pltpu.SMEM((CORES, *near_block.shape), jnp.int32),
            pltpu.SMEM((CORES, 2, *far_region.T.shape), jnp.int32),
            pltpu.SemaphoreType.REGULAR,
            pltpu.SemaphoreType.DMA((2,)),
            pltpu.SemaphoreType.DMA,
            pltpu.SemaphoreType.DMA,
            pltpu.SemaphoreType.DMA,
            pltpu.SemaphoreType.DMA((4,)),
            pltpu.SemaphoreType.DMA,
            pltpu.SemaphoreType.DMA((2,)),
        ],
        compiler_params=pltpu.CompilerParams(collective_id=0, has_side_effects=True),
    )(tiled, near_coef, far_coef, inv_factor, near_block, far_region.T, far_block.T)
    white = white.reshape(tiles, rows, width)
    return jnp.transpose(white, (1, 0, 2)).reshape(rows, columns)


def solution(mesh):
    return jax.shard_map(
        body,
        mesh=mesh,
        in_specs=(
            P("shard", "region"),
            P(("region", "shard"), None, None, None),
            P(("region", "shard"), None, None, None),
            P(("region", "shard"), None, None),
            P(("region", "shard"), None),
            P(("region", "shard"), None),
            P(("region", "shard"), None),
        ),
        out_specs=P("shard", "region"),
        check_vma=False,
    )
```

```python
import functools

import jax
import jax.numpy as jnp
from jax import lax
from jax.experimental import pallas as pl
from jax.experimental.pallas import tpu as pltpu
from jax.sharding import PartitionSpec as P

CORES = 2
RELAY = 1
MESH = pl.DeviceIdType.MESH


def kernel(regions, shards, fields, near_coef, far_coef, inv_factor, near_list,
           region_list, block_list, out, held, relay, early, first, second, middle, third,
           weight, stage, near_of, far_of, ready, list_sem, weight_sem,
           send_sem, gather_sem, land_sem, back_sem, relay_sem):
    blocks, rows, width = held.shape[2:]
    near, far = near_coef.shape[1], far_coef.shape[1]
    members = shards * rows
    chips = regions // CORES
    r, s = lax.axis_index("region"), lax.axis_index("shard")
    core = lax.rem(r, CORES)
    pair = lax.div(r, CORES)
    lead, mate = core == CORES - 1, core == 0
    order = list(reversed(range(1, shards)))
    last = shards - 1
    starts = (0, 1, 2, shards // 2, shards)
    relays, fed = (s == RELAY) & (pair == 0), s == 0
    farthest = (s == last) & (pair == 0)
    close, remote = pl.ds(0, CORES), pl.ds(CORES, regions - CORES)
    via = (CORES - 1, RELAY)

    def odd_of(k):
        return lax.rem(pair + k, chips) * CORES + CORES - 1

    def wait_for(ref, sem):
        pltpu.make_async_copy(ref, ref, sem).wait()

    def send(src, dst, sem, to):
        pltpu.make_async_remote_copy(
            src_ref=src, dst_ref=dst, send_sem=send_sem, recv_sem=sem,
            device_id=to, device_id_type=MESH).start()

    barrier = pltpu.get_barrier_semaphore()
    load = pltpu.make_async_copy(fields, held.at[r], back_sem)

    def parts(half):
        return [(near_list, near_of.at[half], list_sem.at[0]),
                (region_list, far_of.at[half, 0], list_sem.at[1]),
                (block_list, far_of.at[half, 1], list_sem.at[1]),
                (near_coef, weight.at[half, :, pl.ds(0, near)], weight_sem),
                (far_coef, weight.at[half, :, pl.ds(near, far)], weight_sem),
                (inv_factor, weight.at[half, :, near + far], weight_sem)]

    def greet(to):
        pl.semaphore_signal(barrier, inc=1, device_id=to, device_id_type=MESH)

    @pl.when(lead)
    def _():
        @pl.when(relays)
        def _():
            for k in reversed(range(chips)):
                greet((k * CORES, 0))

        for w in order:
            greet((r, s ^ w))
        for k in range(chips):
            greet((lax.rem(pair + k, chips) * CORES, s))
        load.start()

    @pl.when(mate & fed)
    def _():
        load.start()
        pl.semaphore_wait(barrier, chips + 1)
        pl.semaphore_signal(ready, inc=1, device_id=(r + 1, s), device_id_type=MESH)
        load.wait()
        send(held.at[r, last], relay.at[r], relay_sem.at[jnp.minimum(pair, 1)], via)
        for k in reversed(range(chips)):
            send(held.at[r], held.at[r], gather_sem, (odd_of(k), s))


    @pl.when(mate & (s > 0))
    def _():
        pl.semaphore_wait(barrier, chips)
        for k in reversed(range(chips)):
            send(fields, held.at[r], gather_sem, (odd_of(k), s))
        pl.semaphore_signal(ready, inc=1, device_id=(r + 1, s), device_id_type=MESH)

    @pl.when(mate)
    def _():
        for a, b, sem in parts(0):
            send(a, b, sem, (r + 1, s))
        for k in range(chips):
            wait_for(held.at[r], send_sem)
        for a, _, _ in parts(0):
            wait_for(a, send_sem)

        @pl.when(fed)
        def _():
            wait_for(relay.at[0], send_sem)

    @pl.when(lead)
    def _():
        for a, b, sem in parts(1):
            pltpu.make_async_copy(a, b, sem).start()
        load.wait()
        pl.semaphore_wait(ready, 1)

        @pl.when(fed)
        def _():
            send(held.at[r, last], relay.at[r], relay_sem.at[jnp.minimum(pair, 1)], via)

        for k in range(1, chips):
            send(held.at[r], held.at[r], gather_sem, (odd_of(k), s))
        pl.semaphore_wait(barrier, shards - 1)

        @pl.when(relays)
        def _():
            wait_for(relay.at[close], relay_sem.at[0])
            send(relay.at[close], early, relay_sem.at[0], (r, last))
            wait_for(relay.at[remote], relay_sem.at[1])
            send(relay.at[remote], first.at[remote], land_sem.at[0], (r, last))

        wait_for(held.at[pl.ds(0, regions - 1)], gather_sem)
        def spread(dst, sem):
            for w in order:
                send(held.at[:, s ^ w], dst, sem, (r, s ^ w))
            pltpu.make_async_copy(held.at[:, s], dst, sem).start()

        @pl.when(fed)
        def _():
            @pl.when(pair > 0)
            def _():
                send(held.at[:, last], first, land_sem.at[0], (r, last))

            for w in [last - 2, last - 1, *order[3:]]:
                send(held.at[:, w], first, land_sem.at[0], (r, w))
            pltpu.make_async_copy(held.at[:, 0], first, land_sem.at[0]).start()

        batches = (first, second, middle, third)
        for i in range(1, len(batches)):
            @pl.when((s >= starts[i]) & (s < starts[i + 1]))
            def _():
                spread(batches[i].at[:, :, s - starts[i]], land_sem.at[i])

        for ref, sem in ((near_of, list_sem.at[0]), (far_of, list_sem.at[1]), (weight, weight_sem)):
            wait_for(ref, sem)

        indices = [([[near_of[half, b, j] for j in range(near)] for b in range(blocks)],
                    [[(far_of[half, 0, j, b], far_of[half, 1, j, b]) for j in range(far)]
                     for b in range(blocks)])
                   for half in range(CORES)]

        def rows_of(ref, picks, m):
            return jnp.concatenate([ref[k].reshape(m, width) for k in picks], axis=1)

        pairs = range(0, blocks, 2)

        def diagonal(x, y):
            return jnp.concatenate([jnp.concatenate([x, jnp.zeros_like(y)], axis=1),
                                    jnp.concatenate([jnp.zeros_like(x), y], axis=1)], axis=0)

        def padded(x):
            short = -x.shape[0] % 16
            if not short:
                return x
            return jnp.concatenate([x, jnp.zeros((short, x.shape[1]), x.dtype)], axis=0)

        def push(half, kind, slot):
            for i, b in enumerate(pairs):
                if kind == 0 or kind == 2:
                    at = 0 if kind == 0 else near
                    w = [weight[half, c, at:at + 2].reshape(2 * width, width) for c in (b, b + 1)]
                    w = jnp.concatenate(w, axis=1)
                else:
                    at = near - 1 if kind == 1 else near + far
                    w = diagonal(weight[half, b, at], weight[half, b + 1, at])
                pltpu.matmul_push_rhs(w, slot, i)

        def side(ref, half, place, at, m):
            near_at, far_at = indices[half]
            xs = []
            for i, b in enumerate(pairs):
                if at == 1:
                    x = diagonal(*[ref[place, near_at[c][2]].reshape(m, width) for c in (b, b + 1)])
                else:
                    picks = [[(place, k) for k in near_at[c][:2]] if at == 0 else far_at[c]
                             for c in (b, b + 1)]
                    x = jnp.concatenate([rows_of(ref, p, m) for p in picks], axis=0)
                xs.append(padded(x))
            return xs

        def add(accs, xs, slot):
            for i in range(len(xs)):
                pltpu.matmul_acc_lhs(accs[i], xs[i], slot)

        def pops(accs, m):
            return [pltpu.matmul_pop(accs[i])[:2 * m] for i in range(len(pairs))]

        def scoped(f, m):
            high = 2 * m + -2 * m % 16
            pl.run_scoped(f, *[pltpu.ACC(i % len(pairs))((high, 2 * width), jnp.float32)
                               for i in range(2 * len(pairs))])

        def own_of(ref, place, m):
            both = []
            for b in pairs:
                x = [ref[place, c].reshape(m, width).astype(jnp.float32) for c in (b, b + 1)]
                x = jnp.concatenate(x, axis=0)
                both.append(jnp.concatenate([x, x], axis=1))
            return both

        def close_up(accs, half, left, m, slot, start, count):
            shape = left[0].shape
            keep = (lax.broadcasted_iota(jnp.int32, shape, 0) < m) == (
                lax.broadcasted_iota(jnp.int32, shape, 1) < width)
            means = pops(accs, m)
            rest = [padded(jnp.where(keep, x - y, 0.0).astype(jnp.bfloat16))
                    for x, y in zip(left, means)]
            add(accs[len(pairs):], rest, slot)
            for b, white in zip(pairs, pops(accs[len(pairs):], m)):
                white = white.astype(jnp.bfloat16)
                stage[half, pl.ds(start, count), b] = white[:m, :width].reshape(count, rows, width)
                stage[half, pl.ds(start, count), b + 1] = white[m:, width:].reshape(
                    count, rows, width)
            here = r - 1 + half
            for k in range(start, start + count):
                if half == 0:
                    send(stage.at[half, k], out.at[s], back_sem, (here, k))
                else:
                    @pl.when(s != k)
                    def _():
                        send(stage.at[half, k], out.at[s], back_sem, (here, k))

                    @pl.when(s == k)
                    def _():
                        pltpu.make_async_copy(stage.at[half, k], out.at[s], back_sem).start()

        def whiten(ref, sem, start, count):
            m = count * rows
            push(0, 0, 0)
            push(0, 1, 1)
            wait_for(ref, sem)

            def run(*accs):
                for half in range(CORES):
                    here = r - 1 + half
                    if half:
                        push(half, 1, 1)
                    add(accs, side(ref, half, here, 0, m), 0)
                    push(half, 2, 0)
                    add(accs, side(ref, half, here, 1, m), 1)
                    push(half, 3, 1)
                    add(accs, side(ref, half, here, 2, m), 0)
                    if half == 0:
                        push(1, 0, 0)
                    close_up(accs, half, own_of(ref, here, m), m, 1, start, count)

            scoped(run, m)

        @pl.when(farthest)
        def _():
            push(0, 0, 0)
            push(0, 1, 1)
            wait_for(early, relay_sem.at[0])
            first[close] = early[...]

            def run(*accs):
                left = []
                for half in range(CORES):
                    if half:
                        push(half, 0, 0)
                        push(half, 1, 1)
                    add(accs, side(early, half, half, 0, rows), 0)
                    add(accs, side(early, half, half, 1, rows), 1)
                    left.append([x - y for x, y in zip(own_of(early, half, rows), pops(accs, rows))])
                push(0, 2, 0)
                push(0, 3, 1)
                wait_for(first.at[remote], land_sem.at[0])
                add(accs, side(first, 0, 0, 2, rows), 0)
                push(1, 2, 0)
                close_up(accs, 0, left[0], rows, 1, 0, 1)
                push(1, 3, 1)
                add(accs, side(first, 1, 1, 2, rows), 0)
                close_up(accs, 1, left[1], rows, 1, 0, 1)

            scoped(run, rows)

        @pl.when(jnp.logical_not(farthest))
        def _():
            whiten(first, land_sem.at[0], 0, 1)

        for i in range(1, len(batches)):
            whiten(batches[i], land_sem.at[i], starts[i], starts[i + 1] - starts[i])

        for k in range(1, chips):
            wait_for(held.at[r], send_sem)
        wait_for(held.at[:, pl.ds(0, shards - 2)], send_sem)

        @pl.when((s > 0) | (pair > 0))
        def _():
            wait_for(held.at[:, 0], send_sem)

        @pl.when(fed)
        def _():
            wait_for(relay.at[0], send_sem)

        @pl.when(relays)
        def _():
            wait_for(relay, send_sem)

        wait_for(stage.at[0], send_sem)
        wait_for(stage.at[1, pl.ds(0, shards - 1)], send_sem)

    wait_for(out, back_sem)


def body(fields, near_coef, far_coef, inv_factor, near_block, far_region, far_block):
    shards, regions = lax.axis_size("shard"), lax.axis_size("region")
    rows, columns = fields.shape
    blocks, width = near_coef.shape[0], near_coef.shape[3]
    tiles = columns // width
    tiled = jnp.transpose(fields.reshape(rows, tiles, width), (1, 0, 2))
    tiled = tiled.reshape(shards, blocks, rows, width)
    hbm = pl.BlockSpec(memory_space=pl.ANY)
    half = jnp.bfloat16
    white = pl.pallas_call(
        functools.partial(kernel, regions, shards),
        out_shape=pltpu.VMEM(tiled.shape, half),
        in_specs=[hbm] * 7,
        out_specs=pl.BlockSpec(memory_space=pltpu.VMEM),
        scratch_shapes=[
            pltpu.VMEM((regions, shards, blocks, rows, width), half),
            pltpu.VMEM((regions, blocks, rows, width), half),
            pltpu.VMEM((CORES, blocks, rows, width), half),
            pltpu.VMEM((regions, blocks, rows, width), half),
            pltpu.VMEM((regions, blocks, 1, rows, width), half),
            pltpu.VMEM((regions, blocks, shards // 2 - 2, rows, width), half),
            pltpu.VMEM((regions, blocks, shards - shards // 2, rows, width), half),
            pltpu.VMEM((CORES, blocks, near_coef.shape[1] + far_coef.shape[1] + 1, width, width), half),
            pltpu.VMEM((CORES, shards, blocks, rows, width), half),
            pltpu.SMEM((CORES, *near_block.shape), jnp.int32),
            pltpu.SMEM((CORES, 2, *far_region.T.shape), jnp.int32),
            pltpu.SemaphoreType.REGULAR,
            pltpu.SemaphoreType.DMA((2,)),
            pltpu.SemaphoreType.DMA,
            pltpu.SemaphoreType.DMA,
            pltpu.SemaphoreType.DMA,
            pltpu.SemaphoreType.DMA((4,)),
            pltpu.SemaphoreType.DMA,
            pltpu.SemaphoreType.DMA((2,)),
        ],
        compiler_params=pltpu.CompilerParams(collective_id=0, has_side_effects=True),
    )(tiled, near_coef, far_coef, inv_factor, near_block, far_region.T, far_block.T)
    white = white.reshape(tiles, rows, width)
    return jnp.transpose(white, (1, 0, 2)).reshape(rows, columns)


def solution(mesh):
    return jax.shard_map(
        body,
        mesh=mesh,
        in_specs=(
            P("shard", "region"),
            P(("region", "shard"), None, None, None),
            P(("region", "shard"), None, None, None),
            P(("region", "shard"), None, None),
            P(("region", "shard"), None),
            P(("region", "shard"), None),
            P(("region", "shard"), None),
        ),
        out_specs=P("shard", "region"),
        check_vma=False,
    )
```

```python
import functools

import jax
import jax.numpy as jnp
from jax import lax
from jax.experimental import pallas as pl
from jax.experimental.pallas import tpu as pltpu
from jax.sharding import PartitionSpec as P

CORES = 2
RELAY = 1
MESH = pl.DeviceIdType.MESH


def kernel(regions, shards, fields, near_coef, far_coef, inv_factor, near_list,
           region_list, block_list, out, held, relay, early, first, second, middle, third,
           weight, stage, near_of, far_of, ready, list_sem, weight_sem,
           send_sem, gather_sem, land_sem, back_sem, relay_sem):
    blocks, rows, width = held.shape[2:]
    near, far = near_coef.shape[1], far_coef.shape[1]
    members = shards * rows
    chips = regions // CORES
    r, s = lax.axis_index("region"), lax.axis_index("shard")
    core = lax.rem(r, CORES)
    pair = lax.div(r, CORES)
    lead, mate = core == CORES - 1, core == 0
    order = list(reversed(range(1, shards)))
    last = shards - 1
    starts = (0, 1, 2, shards // 2, shards)
    relays, fed = (s == RELAY) & (pair == 0), s == 0
    farthest = (s == last) & (pair == 0)
    halves = (pl.ds(shards // 2, shards // 2), pl.ds(0, shards // 2))
    close, remote = pl.ds(0, CORES), pl.ds(CORES, regions - CORES)
    via = (CORES - 1, RELAY)

    def odd_of(k):
        return lax.rem(pair + k, chips) * CORES + CORES - 1

    def wait_for(ref, sem):
        pltpu.make_async_copy(ref, ref, sem).wait()

    def send(src, dst, sem, to):
        pltpu.make_async_remote_copy(
            src_ref=src, dst_ref=dst, send_sem=send_sem, recv_sem=sem,
            device_id=to, device_id_type=MESH).start()

    barrier = pltpu.get_barrier_semaphore()
    load = pltpu.make_async_copy(fields, held.at[r], back_sem)

    def parts(half):
        return [(near_list, near_of.at[half], list_sem.at[0]),
                (region_list, far_of.at[half, 0], list_sem.at[1]),
                (block_list, far_of.at[half, 1], list_sem.at[1]),
                (near_coef, weight.at[half, :, pl.ds(0, near)], weight_sem),
                (far_coef, weight.at[half, :, pl.ds(near, far)], weight_sem),
                (inv_factor, weight.at[half, :, near + far], weight_sem)]

    def greet(to):
        pl.semaphore_signal(barrier, inc=1, device_id=to, device_id_type=MESH)

    @pl.when(lead)
    def _():
        @pl.when(relays)
        def _():
            for k in reversed(range(chips)):
                greet((k * CORES, 0))

        for w in order:
            greet((r, s ^ w))
        for k in range(chips):
            greet((lax.rem(pair + k, chips) * CORES, s))
        load.start()

    @pl.when(mate & fed)
    def _():
        load.start()
        pl.semaphore_wait(barrier, chips + 1)
        pl.semaphore_signal(ready, inc=1, device_id=(r + 1, s), device_id_type=MESH)
        load.wait()
        @pl.when(pair == 0)
        def _():
            send(held.at[r, last], relay.at[r], relay_sem, via)

        @pl.when(pair > 0)
        def _():
            send(held.at[r, last], relay.at[r], land_sem.at[RELAY], via)

        for i, cut in enumerate(halves):
            for k in reversed(range(chips)):
                send(held.at[r, cut], held.at[r, cut], gather_sem.at[i], (odd_of(k), s))


    @pl.when(mate & (s > 0))
    def _():
        pl.semaphore_wait(barrier, chips)
        for k in reversed(range(chips)):
            send(fields, held.at[r], gather_sem.at[0], (odd_of(k), s))
        pl.semaphore_signal(ready, inc=1, device_id=(r + 1, s), device_id_type=MESH)

    @pl.when(mate)
    def _():
        for a, b, sem in parts(0):
            send(a, b, sem, (r + 1, s))
        for k in range(chips):
            wait_for(held.at[r], send_sem)
        for a, _, _ in parts(0):
            wait_for(a, send_sem)

        @pl.when(fed)
        def _():
            wait_for(relay.at[0], send_sem)

    @pl.when(lead)
    def _():
        for a, b, sem in parts(1):
            pltpu.make_async_copy(a, b, sem).start()
        load.wait()
        pl.semaphore_wait(ready, 1)

        @pl.when(fed)
        def _():
            @pl.when(pair == 0)
            def _():
                send(held.at[r, last], relay.at[r], relay_sem, via)

            @pl.when(pair > 0)
            def _():
                send(held.at[r, last], relay.at[r], land_sem.at[RELAY], via)

        @pl.when(fed)
        def _():
            for i, cut in enumerate(halves):
                for k in range(1, chips):
                    send(held.at[r, cut], held.at[r, cut], gather_sem.at[i], (odd_of(k), s))

        @pl.when(s > 0)
        def _():
            for k in range(1, chips):
                send(held.at[r], held.at[r], gather_sem.at[0], (odd_of(k), s))

        pl.semaphore_wait(barrier, shards - 1)

        @pl.when(relays)
        def _():
            wait_for(relay.at[close], relay_sem)
            send(relay.at[close], early, relay_sem, (r, last))
            wait_for(relay.at[remote], land_sem.at[RELAY])
            send(relay.at[remote], first.at[remote], land_sem.at[0], (r, last))

        @pl.when(s > 0)
        def _():
            wait_for(held.at[pl.ds(0, regions - 1)], gather_sem.at[0])

        def spread(dst, sem):
            for w in order:
                send(held.at[:, s ^ w], dst, sem, (r, s ^ w))
            pltpu.make_async_copy(held.at[:, s], dst, sem).start()

        @pl.when(fed)
        def _():
            wait_for(held.at[pl.ds(0, regions - 1), halves[0]], gather_sem.at[0])

            @pl.when(pair > 0)
            def _():
                send(held.at[:, last], first, land_sem.at[0], (r, last))

            ahead = [last - 2, last - 1, *order[3:]]
            for w in [w for w in ahead if w >= shards // 2]:
                send(held.at[:, w], first, land_sem.at[0], (r, w))
            wait_for(held.at[pl.ds(0, regions - 1), halves[1]], gather_sem.at[1])
            for w in [w for w in ahead if w < shards // 2]:
                send(held.at[:, w], first, land_sem.at[0], (r, w))
            pltpu.make_async_copy(held.at[:, 0], first, land_sem.at[0]).start()

        batches = (first, second, middle, third)
        for i in range(1, len(batches)):
            @pl.when((s >= starts[i]) & (s < starts[i + 1]))
            def _():
                spread(batches[i].at[:, :, s - starts[i]], land_sem.at[i])

        for ref, sem in ((near_of, list_sem.at[0]), (far_of, list_sem.at[1]), (weight, weight_sem)):
            wait_for(ref, sem)

        indices = [([[near_of[half, b, j] for j in range(near)] for b in range(blocks)],
                    [[(far_of[half, 0, j, b], far_of[half, 1, j, b]) for j in range(far)]
                     for b in range(blocks)])
                   for half in range(CORES)]

        def rows_of(ref, picks, m):
            return jnp.concatenate([ref[k].reshape(m, width) for k in picks], axis=1)

        pairs = range(0, blocks, 2)

        def diagonal(x, y):
            return jnp.concatenate([jnp.concatenate([x, jnp.zeros_like(y)], axis=1),
                                    jnp.concatenate([jnp.zeros_like(x), y], axis=1)], axis=0)

        def padded(x):
            short = -x.shape[0] % 16
            if not short:
                return x
            return jnp.concatenate([x, jnp.zeros((short, x.shape[1]), x.dtype)], axis=0)

        def push(half, kind, slot):
            for i, b in enumerate(pairs):
                if kind == 0 or kind == 2:
                    at = 0 if kind == 0 else near
                    w = [weight[half, c, at:at + 2].reshape(2 * width, width) for c in (b, b + 1)]
                    w = jnp.concatenate(w, axis=1)
                else:
                    at = near - 1 if kind == 1 else near + far
                    w = diagonal(weight[half, b, at], weight[half, b + 1, at])
                pltpu.matmul_push_rhs(w, slot, i)

        def side(ref, half, place, at, m):
            near_at, far_at = indices[half]
            xs = []
            for i, b in enumerate(pairs):
                if at == 1:
                    x = diagonal(*[ref[place, near_at[c][2]].reshape(m, width) for c in (b, b + 1)])
                else:
                    picks = [[(place, k) for k in near_at[c][:2]] if at == 0 else far_at[c]
                             for c in (b, b + 1)]
                    x = jnp.concatenate([rows_of(ref, p, m) for p in picks], axis=0)
                xs.append(padded(x))
            return xs

        def add(accs, xs, slot):
            for i in range(len(xs)):
                pltpu.matmul_acc_lhs(accs[i], xs[i], slot)

        def pops(accs, m):
            return [pltpu.matmul_pop(accs[i])[:2 * m] for i in range(len(pairs))]

        def scoped(f, m):
            high = 2 * m + -2 * m % 16
            pl.run_scoped(f, *[pltpu.ACC(i % len(pairs))((high, 2 * width), jnp.float32)
                               for i in range(2 * len(pairs))])

        def own_of(ref, place, m):
            both = []
            for b in pairs:
                x = [ref[place, c].reshape(m, width).astype(jnp.float32) for c in (b, b + 1)]
                x = jnp.concatenate(x, axis=0)
                both.append(jnp.concatenate([x, x], axis=1))
            return both

        def close_up(accs, half, left, m, slot, start, count):
            shape = left[0].shape
            keep = (lax.broadcasted_iota(jnp.int32, shape, 0) < m) == (
                lax.broadcasted_iota(jnp.int32, shape, 1) < width)
            means = pops(accs, m)
            rest = [padded(jnp.where(keep, x - y, 0.0).astype(jnp.bfloat16))
                    for x, y in zip(left, means)]
            add(accs[len(pairs):], rest, slot)
            for b, white in zip(pairs, pops(accs[len(pairs):], m)):
                white = white.astype(jnp.bfloat16)
                stage[half, pl.ds(start, count), b] = white[:m, :width].reshape(count, rows, width)
                stage[half, pl.ds(start, count), b + 1] = white[m:, width:].reshape(
                    count, rows, width)
            here = r - 1 + half
            for k in range(start, start + count):
                if half == 0:
                    send(stage.at[half, k], out.at[s], back_sem, (here, k))
                else:
                    @pl.when(s != k)
                    def _():
                        send(stage.at[half, k], out.at[s], back_sem, (here, k))

                    @pl.when(s == k)
                    def _():
                        pltpu.make_async_copy(stage.at[half, k], out.at[s], back_sem).start()

        def whiten(ref, sem, start, count):
            m = count * rows
            push(0, 0, 0)
            push(0, 1, 1)
            wait_for(ref, sem)

            def run(*accs):
                for half in range(CORES):
                    here = r - 1 + half
                    if half:
                        push(half, 1, 1)
                    add(accs, side(ref, half, here, 0, m), 0)
                    push(half, 2, 0)
                    add(accs, side(ref, half, here, 1, m), 1)
                    push(half, 3, 1)
                    add(accs, side(ref, half, here, 2, m), 0)
                    if half == 0:
                        push(1, 0, 0)
                    close_up(accs, half, own_of(ref, here, m), m, 1, start, count)

            scoped(run, m)

        @pl.when(farthest)
        def _():
            push(0, 0, 0)
            push(0, 1, 1)
            wait_for(early, relay_sem)
            first[close] = early[...]

            def run(*accs):
                left = []
                for half in range(CORES):
                    if half:
                        push(half, 0, 0)
                        push(half, 1, 1)
                    add(accs, side(early, half, half, 0, rows), 0)
                    add(accs, side(early, half, half, 1, rows), 1)
                    left.append([x - y for x, y in zip(own_of(early, half, rows), pops(accs, rows))])
                push(0, 2, 0)
                push(0, 3, 1)
                wait_for(first.at[remote], land_sem.at[0])
                add(accs, side(first, 0, 0, 2, rows), 0)
                push(1, 2, 0)
                close_up(accs, 0, left[0], rows, 1, 0, 1)
                push(1, 3, 1)
                add(accs, side(first, 1, 1, 2, rows), 0)
                close_up(accs, 1, left[1], rows, 1, 0, 1)

            scoped(run, rows)

        @pl.when(jnp.logical_not(farthest))
        def _():
            whiten(first, land_sem.at[0], 0, 1)

        for i in range(1, len(batches)):
            whiten(batches[i], land_sem.at[i], starts[i], starts[i + 1] - starts[i])

        for k in range(1, chips):
            wait_for(held.at[r], send_sem)
        wait_for(held.at[:, pl.ds(0, shards - 2)], send_sem)

        @pl.when((s > 0) | (pair > 0))
        def _():
            wait_for(held.at[:, 0], send_sem)

        @pl.when(fed)
        def _():
            wait_for(relay.at[0], send_sem)

        @pl.when(relays)
        def _():
            wait_for(relay, send_sem)

        wait_for(stage.at[0], send_sem)
        wait_for(stage.at[1, pl.ds(0, shards - 1)], send_sem)

    wait_for(out, back_sem)


def body(fields, near_coef, far_coef, inv_factor, near_block, far_region, far_block):
    shards, regions = lax.axis_size("shard"), lax.axis_size("region")
    rows, columns = fields.shape
    blocks, width = near_coef.shape[0], near_coef.shape[3]
    tiles = columns // width
    tiled = jnp.transpose(fields.reshape(rows, tiles, width), (1, 0, 2))
    tiled = tiled.reshape(shards, blocks, rows, width)
    hbm = pl.BlockSpec(memory_space=pl.ANY)
    half = jnp.bfloat16
    white = pl.pallas_call(
        functools.partial(kernel, regions, shards),
        out_shape=pltpu.VMEM(tiled.shape, half),
        in_specs=[hbm] * 7,
        out_specs=pl.BlockSpec(memory_space=pltpu.VMEM),
        scratch_shapes=[
            pltpu.VMEM((regions, shards, blocks, rows, width), half),
            pltpu.VMEM((regions, blocks, rows, width), half),
            pltpu.VMEM((CORES, blocks, rows, width), half),
            pltpu.VMEM((regions, blocks, rows, width), half),
            pltpu.VMEM((regions, blocks, 1, rows, width), half),
            pltpu.VMEM((regions, blocks, shards // 2 - 2, rows, width), half),
            pltpu.VMEM((regions, blocks, shards - shards // 2, rows, width), half),
            pltpu.VMEM((CORES, blocks, near_coef.shape[1] + far_coef.shape[1] + 1, width, width), half),
            pltpu.VMEM((CORES, shards, blocks, rows, width), half),
            pltpu.SMEM((CORES, *near_block.shape), jnp.int32),
            pltpu.SMEM((CORES, 2, *far_region.T.shape), jnp.int32),
            pltpu.SemaphoreType.REGULAR,
            pltpu.SemaphoreType.DMA((2,)),
            pltpu.SemaphoreType.DMA,
            pltpu.SemaphoreType.DMA,
            pltpu.SemaphoreType.DMA((2,)),
            pltpu.SemaphoreType.DMA((4,)),
            pltpu.SemaphoreType.DMA,
            pltpu.SemaphoreType.DMA,
        ],
        compiler_params=pltpu.CompilerParams(collective_id=0, has_side_effects=True),
    )(tiled, near_coef, far_coef, inv_factor, near_block, far_region.T, far_block.T)
    white = white.reshape(tiles, rows, width)
    return jnp.transpose(white, (1, 0, 2)).reshape(rows, columns)


def solution(mesh):
    return jax.shard_map(
        body,
        mesh=mesh,
        in_specs=(
            P("shard", "region"),
            P(("region", "shard"), None, None, None),
            P(("region", "shard"), None, None, None),
            P(("region", "shard"), None, None),
            P(("region", "shard"), None),
            P(("region", "shard"), None),
            P(("region", "shard"), None),
        ),
        out_specs=P("shard", "region"),
        check_vma=False,
    )
```

```python
import functools

import jax
import jax.numpy as jnp
from jax import lax
from jax.experimental import pallas as pl
from jax.experimental.pallas import tpu as pltpu
from jax.sharding import PartitionSpec as P

CORES = 2
RELAY = 1
MESH = pl.DeviceIdType.MESH


def kernel(regions, shards, fields, near_coef, far_coef, inv_factor, near_list,
           region_list, block_list, out, held, relay, early, first, second, middle, third,
           weight, stage, near_of, far_of, ready, list_sem, weight_sem,
           send_sem, gather_sem, land_sem, back_sem, relay_sem):
    blocks, rows, width = held.shape[2:]
    near, far = near_coef.shape[1], far_coef.shape[1]
    members = shards * rows
    chips = regions // CORES
    r, s = lax.axis_index("region"), lax.axis_index("shard")
    core = lax.rem(r, CORES)
    pair = lax.div(r, CORES)
    lead, mate = core == CORES - 1, core == 0
    order = list(reversed(range(1, shards)))
    last = shards - 1
    starts = (0, 1, 2, shards // 2, shards)
    relays, fed = (s == RELAY) & (pair == 0), s == 0
    farthest = (s == last) & (pair == 0)
    halves = (pl.ds(shards // 2, shards // 2), pl.ds(0, shards // 2))
    close, remote = pl.ds(0, CORES), pl.ds(CORES, regions - CORES)
    via = (CORES - 1, RELAY)

    def odd_of(k):
        return lax.rem(pair + k, chips) * CORES + CORES - 1

    def wait_for(ref, sem):
        pltpu.make_async_copy(ref, ref, sem).wait()

    def send(src, dst, sem, to):
        pltpu.make_async_remote_copy(
            src_ref=src, dst_ref=dst, send_sem=send_sem, recv_sem=sem,
            device_id=to, device_id_type=MESH).start()

    barrier = pltpu.get_barrier_semaphore()
    load = pltpu.make_async_copy(fields, held.at[r], back_sem)

    def parts(half):
        return [(near_list, near_of.at[half], list_sem.at[0]),
                (region_list, far_of.at[half, 0], list_sem.at[1]),
                (block_list, far_of.at[half, 1], list_sem.at[1]),
                (near_coef, weight.at[half, :, pl.ds(0, near)], weight_sem),
                (far_coef, weight.at[half, :, pl.ds(near, far)], weight_sem),
                (inv_factor, weight.at[half, :, near + far], weight_sem)]

    def greet(to):
        pl.semaphore_signal(barrier, inc=1, device_id=to, device_id_type=MESH)

    @pl.when(lead)
    def _():
        @pl.when(relays)
        def _():
            for k in reversed(range(chips)):
                greet((k * CORES, 0))

        for w in order:
            greet((r, s ^ w))
        for k in range(chips):
            greet((lax.rem(pair + k, chips) * CORES, s))
        load.start()

    @pl.when(mate & fed)
    def _():
        load.start()
        pl.semaphore_wait(barrier, chips + 1)
        pl.semaphore_signal(ready, inc=1, device_id=(r + 1, s), device_id_type=MESH)
        load.wait()
        @pl.when(pair == 0)
        def _():
            send(held.at[r, last], relay.at[r], relay_sem, via)

        @pl.when(pair > 0)
        def _():
            send(held.at[r, last], relay.at[r], land_sem.at[RELAY], via)

        for i, cut in enumerate(halves):
            for k in reversed(range(chips)):
                send(held.at[r, cut], held.at[r, cut], gather_sem.at[i], (odd_of(k), s))


    @pl.when(mate & (s > 0))
    def _():
        pl.semaphore_wait(barrier, chips)
        for k in reversed(range(chips)):
            send(fields, held.at[r], gather_sem.at[0], (odd_of(k), s))
        pl.semaphore_signal(ready, inc=1, device_id=(r + 1, s), device_id_type=MESH)

    @pl.when(mate)
    def _():
        for a, b, sem in parts(0):
            send(a, b, sem, (r + 1, s))
        for k in range(chips):
            wait_for(held.at[r], send_sem)
        for a, _, _ in parts(0):
            wait_for(a, send_sem)

        @pl.when(fed)
        def _():
            wait_for(relay.at[0], send_sem)

    @pl.when(lead)
    def _():
        for a, b, sem in parts(1):
            pltpu.make_async_copy(a, b, sem).start()
        load.wait()
        pl.semaphore_wait(ready, 1)

        @pl.when(fed)
        def _():
            @pl.when(pair == 0)
            def _():
                send(held.at[r, last], relay.at[r], relay_sem, via)

            @pl.when(pair > 0)
            def _():
                send(held.at[r, last], relay.at[r], land_sem.at[RELAY], via)

        @pl.when(fed)
        def _():
            for i, cut in enumerate(halves):
                for k in range(1, chips):
                    send(held.at[r, cut], held.at[r, cut], gather_sem.at[i], (odd_of(k), s))

        @pl.when(s > 0)
        def _():
            for k in range(1, chips):
                send(held.at[r], held.at[r], gather_sem.at[0], (odd_of(k), s))

        pl.semaphore_wait(barrier, shards - 1)

        @pl.when(relays)
        def _():
            wait_for(relay.at[close], relay_sem)
            send(relay.at[close], early, relay_sem, (r, last))
            wait_for(relay.at[remote], land_sem.at[RELAY])
            send(relay.at[remote], first.at[remote], land_sem.at[0], (r, last))

        @pl.when(s > 0)
        def _():
            wait_for(held.at[pl.ds(0, regions - 1)], gather_sem.at[0])

        def spread(dst, sem):
            for w in order:
                send(held.at[:, s ^ w], dst, sem, (r, s ^ w))
            pltpu.make_async_copy(held.at[:, s], dst, sem).start()

        @pl.when(fed)
        def _():
            wait_for(held.at[pl.ds(0, regions - 1), halves[0]], gather_sem.at[0])

            @pl.when(pair > 0)
            def _():
                send(held.at[:, last], first, land_sem.at[0], (r, last))

            ahead = [last - 2, last - 1, *order[3:]]
            for w in [w for w in ahead if w >= shards // 2]:
                send(held.at[:, w], first, land_sem.at[0], (r, w))
            wait_for(held.at[pl.ds(0, regions - 1), halves[1]], gather_sem.at[1])
            for w in [w for w in ahead if w < shards // 2]:
                send(held.at[:, w], first, land_sem.at[0], (r, w))
            pltpu.make_async_copy(held.at[:, 0], first, land_sem.at[0]).start()

        batches = (first, second, middle, third)
        for i in range(1, len(batches)):
            @pl.when((s >= starts[i]) & (s < starts[i + 1]))
            def _():
                spread(batches[i].at[:, :, s - starts[i]], land_sem.at[i])

        for ref, sem in ((near_of, list_sem.at[0]), (far_of, list_sem.at[1]), (weight, weight_sem)):
            wait_for(ref, sem)

        indices = [([[near_of[half, b, j] for j in range(near)] for b in range(blocks)],
                    [[(far_of[half, 0, j, b], far_of[half, 1, j, b]) for j in range(far)]
                     for b in range(blocks)])
                   for half in range(CORES)]

        def rows_of(ref, picks, m):
            return jnp.concatenate([ref[k].reshape(m, width) for k in picks], axis=1)

        pairs = range(0, blocks, 2)

        def diagonal(x, y):
            return jnp.concatenate([jnp.concatenate([x, jnp.zeros_like(y)], axis=1),
                                    jnp.concatenate([jnp.zeros_like(x), y], axis=1)], axis=0)

        def padded(x):
            short = -x.shape[0] % 16
            if not short:
                return x
            return jnp.concatenate([x, jnp.zeros((short, x.shape[1]), x.dtype)], axis=0)

        def push(half, kind, slot):
            for i, b in enumerate(pairs):
                if kind == 0 or kind == 2:
                    at = 0 if kind == 0 else near
                    w = [weight[half, c, at:at + 2].reshape(2 * width, width) for c in (b, b + 1)]
                    w = jnp.concatenate(w, axis=1)
                else:
                    at = near - 1 if kind == 1 else near + far
                    w = diagonal(weight[half, b, at], weight[half, b + 1, at])
                pltpu.matmul_push_rhs(w, slot, i)

        def side(ref, half, place, at, m):
            near_at, far_at = indices[half]
            xs = []
            for i, b in enumerate(pairs):
                if at == 1:
                    x = diagonal(*[ref[place, near_at[c][2]].reshape(m, width) for c in (b, b + 1)])
                else:
                    picks = [[(place, k) for k in near_at[c][:2]] if at == 0 else far_at[c]
                             for c in (b, b + 1)]
                    x = jnp.concatenate([rows_of(ref, p, m) for p in picks], axis=0)
                xs.append(padded(x))
            return xs

        def add(accs, xs, slot):
            for i in range(len(xs)):
                pltpu.matmul_acc_lhs(accs[i], xs[i], slot)

        def pops(accs, m):
            return [pltpu.matmul_pop(accs[i])[:2 * m] for i in range(len(pairs))]

        def scoped(f, m):
            high = 2 * m + -2 * m % 16
            pl.run_scoped(f, *[pltpu.ACC(i % len(pairs))((high, 2 * width), jnp.float32)
                               for i in range(2 * len(pairs))])

        def own_of(ref, place, m):
            both = []
            for b in pairs:
                x = [ref[place, c].reshape(m, width).astype(jnp.float32) for c in (b, b + 1)]
                x = jnp.concatenate(x, axis=0)
                both.append(jnp.concatenate([x, x], axis=1))
            return both

        def close_up(accs, half, left, m, slot, start, count):
            shape = left[0].shape
            keep = (lax.broadcasted_iota(jnp.int32, shape, 0) < m) == (
                lax.broadcasted_iota(jnp.int32, shape, 1) < width)
            means = pops(accs, m)
            rest = [padded(jnp.where(keep, x - y, 0.0).astype(jnp.bfloat16))
                    for x, y in zip(left, means)]
            add(accs[len(pairs):], rest, slot)
            for b, white in zip(pairs, pops(accs[len(pairs):], m)):
                white = white.astype(jnp.bfloat16)
                stage[half, pl.ds(start, count), b] = white[:m, :width].reshape(count, rows, width)
                stage[half, pl.ds(start, count), b + 1] = white[m:, width:].reshape(
                    count, rows, width)
            here = r - 1 + half
            for k in range(start, start + count):
                if half == 0:
                    send(stage.at[half, k], out.at[s], back_sem, (here, k))
                else:
                    @pl.when(s != k)
                    def _():
                        send(stage.at[half, k], out.at[s], back_sem, (here, k))

                    @pl.when(s == k)
                    def _():
                        pltpu.make_async_copy(stage.at[half, k], out.at[s], back_sem).start()

        def whiten(ref, sem, start, count):
            m = count * rows
            push(0, 0, 0)
            push(0, 1, 1)
            wait_for(ref, sem)

            def run(*accs):
                for half in range(CORES):
                    here = r - 1 + half
                    if half:
                        push(half, 1, 1)
                    add(accs, side(ref, half, here, 0, m), 0)
                    push(half, 2, 0)
                    add(accs, side(ref, half, here, 1, m), 1)
                    push(half, 3, 1)
                    add(accs, side(ref, half, here, 2, m), 0)
                    if half == 0:
                        push(1, 0, 0)
                    close_up(accs, half, own_of(ref, here, m), m, 1, start, count)

            scoped(run, m)

        @pl.when(farthest)
        def _():
            push(0, 0, 0)
            push(0, 1, 1)
            wait_for(early, relay_sem)
            first[close] = early[...]

            def run(*accs):
                left = []
                for half in range(CORES):
                    if half:
                        push(half, 0, 0)
                        push(half, 1, 1)
                    add(accs, side(early, half, half, 0, rows), 0)
                    add(accs, side(early, half, half, 1, rows), 1)
                    left.append([x - y for x, y in zip(own_of(early, half, rows), pops(accs, rows))])
                push(0, 2, 0)
                push(0, 3, 1)
                wait_for(first.at[remote], land_sem.at[0])
                add(accs, side(first, 0, 0, 2, rows), 0)
                close_up(accs, 0, left[0], rows, 1, 0, 1)
                push(1, 2, 0)
                push(1, 3, 1)
                add(accs, side(first, 1, 1, 2, rows), 0)
                close_up(accs, 1, left[1], rows, 1, 0, 1)

            scoped(run, rows)

        @pl.when(jnp.logical_not(farthest))
        def _():
            whiten(first, land_sem.at[0], 0, 1)

        for i in range(1, len(batches)):
            whiten(batches[i], land_sem.at[i], starts[i], starts[i + 1] - starts[i])

        for k in range(1, chips):
            wait_for(held.at[r], send_sem)
        wait_for(held.at[:, pl.ds(0, shards - 2)], send_sem)

        @pl.when((s > 0) | (pair > 0))
        def _():
            wait_for(held.at[:, 0], send_sem)

        @pl.when(fed)
        def _():
            wait_for(relay.at[0], send_sem)

        @pl.when(relays)
        def _():
            wait_for(relay, send_sem)

        wait_for(stage.at[0], send_sem)
        wait_for(stage.at[1, pl.ds(0, shards - 1)], send_sem)

    wait_for(out, back_sem)


def body(fields, near_coef, far_coef, inv_factor, near_block, far_region, far_block):
    shards, regions = lax.axis_size("shard"), lax.axis_size("region")
    rows, columns = fields.shape
    blocks, width = near_coef.shape[0], near_coef.shape[3]
    tiles = columns // width
    tiled = jnp.transpose(fields.reshape(rows, tiles, width), (1, 0, 2))
    tiled = tiled.reshape(shards, blocks, rows, width)
    hbm = pl.BlockSpec(memory_space=pl.ANY)
    half = jnp.bfloat16
    white = pl.pallas_call(
        functools.partial(kernel, regions, shards),
        out_shape=pltpu.VMEM(tiled.shape, half),
        in_specs=[hbm] * 7,
        out_specs=pl.BlockSpec(memory_space=pltpu.VMEM),
        scratch_shapes=[
            pltpu.VMEM((regions, shards, blocks, rows, width), half),
            pltpu.VMEM((regions, blocks, rows, width), half),
            pltpu.VMEM((CORES, blocks, rows, width), half),
            pltpu.VMEM((regions, blocks, rows, width), half),
            pltpu.VMEM((regions, blocks, 1, rows, width), half),
            pltpu.VMEM((regions, blocks, shards // 2 - 2, rows, width), half),
            pltpu.VMEM((regions, blocks, shards - shards // 2, rows, width), half),
            pltpu.VMEM((CORES, blocks, near_coef.shape[1] + far_coef.shape[1] + 1, width, width), half),
            pltpu.VMEM((CORES, shards, blocks, rows, width), half),
            pltpu.SMEM((CORES, *near_block.shape), jnp.int32),
            pltpu.SMEM((CORES, 2, *far_region.T.shape), jnp.int32),
            pltpu.SemaphoreType.REGULAR,
            pltpu.SemaphoreType.DMA((2,)),
            pltpu.SemaphoreType.DMA,
            pltpu.SemaphoreType.DMA,
            pltpu.SemaphoreType.DMA((2,)),
            pltpu.SemaphoreType.DMA((4,)),
            pltpu.SemaphoreType.DMA,
            pltpu.SemaphoreType.DMA,
        ],
        compiler_params=pltpu.CompilerParams(collective_id=0, has_side_effects=True),
    )(tiled, near_coef, far_coef, inv_factor, near_block, far_region.T, far_block.T)
    white = white.reshape(tiles, rows, width)
    return jnp.transpose(white, (1, 0, 2)).reshape(rows, columns)


def solution(mesh):
    return jax.shard_map(
        body,
        mesh=mesh,
        in_specs=(
            P("shard", "region"),
            P(("region", "shard"), None, None, None),
            P(("region", "shard"), None, None, None),
            P(("region", "shard"), None, None),
            P(("region", "shard"), None),
            P(("region", "shard"), None),
            P(("region", "shard"), None),
        ),
        out_specs=P("shard", "region"),
        check_vma=False,
    )
```

```python
import functools

import jax
import jax.numpy as jnp
from jax import lax
from jax.experimental import pallas as pl
from jax.experimental.pallas import tpu as pltpu
from jax.sharding import PartitionSpec as P

CORES = 2
RELAY = 1
MESH = pl.DeviceIdType.MESH


def kernel(regions, shards, fields, near_coef, far_coef, inv_factor, near_list,
           region_list, block_list, out, held, relay, early, first, second, middle, third,
           weight, stage, near_of, far_of, ready, list_sem, weight_sem,
           send_sem, gather_sem, land_sem, back_sem, relay_sem):
    blocks, rows, width = held.shape[2:]
    near, far = near_coef.shape[1], far_coef.shape[1]
    members = shards * rows
    chips = regions // CORES
    r, s = lax.axis_index("region"), lax.axis_index("shard")
    core = lax.rem(r, CORES)
    pair = lax.div(r, CORES)
    lead, mate = core == CORES - 1, core == 0
    order = list(reversed(range(1, shards)))
    last = shards - 1
    starts = (0, 1, 2, shards // 2, shards)
    relays, fed = (s == RELAY) & (pair == 0), s == 0
    farthest = (s == last) & (pair == 0)
    halves = (pl.ds(shards // 2, shards // 2), pl.ds(0, shards // 2))
    close, remote = pl.ds(0, CORES), pl.ds(CORES, regions - CORES)
    via = (CORES - 1, RELAY)

    def odd_of(k):
        return lax.rem(pair + k, chips) * CORES + CORES - 1

    def wait_for(ref, sem):
        pltpu.make_async_copy(ref, ref, sem).wait()

    def send(src, dst, sem, to):
        pltpu.make_async_remote_copy(
            src_ref=src, dst_ref=dst, send_sem=send_sem, recv_sem=sem,
            device_id=to, device_id_type=MESH).start()

    barrier = pltpu.get_barrier_semaphore()
    load = pltpu.make_async_copy(fields, held.at[r], back_sem)

    def parts(half):
        return [(near_list, near_of.at[half], list_sem.at[0]),
                (region_list, far_of.at[half, 0], list_sem.at[1]),
                (block_list, far_of.at[half, 1], list_sem.at[1]),
                (near_coef, weight.at[half, :, pl.ds(0, near)], weight_sem),
                (far_coef, weight.at[half, :, pl.ds(near, far)], weight_sem),
                (inv_factor, weight.at[half, :, near + far], weight_sem)]

    def greet(to):
        pl.semaphore_signal(barrier, inc=1, device_id=to, device_id_type=MESH)

    @pl.when(lead)
    def _():
        @pl.when(relays)
        def _():
            for k in reversed(range(chips)):
                greet((k * CORES, 0))

        for w in order:
            greet((r, s ^ w))
        for k in range(chips):
            greet((lax.rem(pair + k, chips) * CORES, s))
        load.start()

    @pl.when(mate & fed)
    def _():
        tile = pltpu.make_async_copy(fields.at[last], held.at[r, last], back_sem)
        others = pl.ds(0, last)
        bulk = pltpu.make_async_copy(fields.at[others], held.at[r, others], gather_sem.at[0])
        tile.start()
        bulk.start()
        pl.semaphore_wait(barrier, chips + 1)
        pl.semaphore_signal(ready, inc=1, device_id=(r + 1, s), device_id_type=MESH)
        tile.wait()
        @pl.when(pair == 0)
        def _():
            send(held.at[r, last], relay.at[r], relay_sem, via)

        @pl.when(pair > 0)
        def _():
            send(held.at[r, last], relay.at[r], land_sem.at[RELAY], via)

        bulk.wait()
        for i, cut in enumerate(halves):
            for k in reversed(range(chips)):
                send(held.at[r, cut], held.at[r, cut], gather_sem.at[i], (odd_of(k), s))


    @pl.when(mate & (s > 0))
    def _():
        pl.semaphore_wait(barrier, chips)
        for k in reversed(range(chips)):
            send(fields, held.at[r], gather_sem.at[0], (odd_of(k), s))
        pl.semaphore_signal(ready, inc=1, device_id=(r + 1, s), device_id_type=MESH)

    @pl.when(mate)
    def _():
        for a, b, sem in parts(0):
            send(a, b, sem, (r + 1, s))
        for k in range(chips):
            wait_for(held.at[r], send_sem)
        for a, _, _ in parts(0):
            wait_for(a, send_sem)

        @pl.when(fed)
        def _():
            wait_for(relay.at[0], send_sem)

    @pl.when(lead)
    def _():
        for a, b, sem in parts(1):
            pltpu.make_async_copy(a, b, sem).start()
        load.wait()
        pl.semaphore_wait(ready, 1)

        @pl.when(fed)
        def _():
            @pl.when(pair == 0)
            def _():
                send(held.at[r, last], relay.at[r], relay_sem, via)

            @pl.when(pair > 0)
            def _():
                send(held.at[r, last], relay.at[r], land_sem.at[RELAY], via)

        @pl.when(fed)
        def _():
            for i, cut in enumerate(halves):
                for k in range(1, chips):
                    send(held.at[r, cut], held.at[r, cut], gather_sem.at[i], (odd_of(k), s))

        @pl.when(s > 0)
        def _():
            for k in range(1, chips):
                send(held.at[r], held.at[r], gather_sem.at[0], (odd_of(k), s))

        pl.semaphore_wait(barrier, shards - 1)

        @pl.when(relays)
        def _():
            wait_for(relay.at[close], relay_sem)
            send(relay.at[close], early, relay_sem, (r, last))
            wait_for(relay.at[remote], land_sem.at[RELAY])
            send(relay.at[remote], first.at[remote], land_sem.at[0], (r, last))

        @pl.when(s > 0)
        def _():
            wait_for(held.at[pl.ds(0, regions - 1)], gather_sem.at[0])

        def spread(dst, sem):
            for w in order:
                send(held.at[:, s ^ w], dst, sem, (r, s ^ w))
            pltpu.make_async_copy(held.at[:, s], dst, sem).start()

        @pl.when(fed)
        def _():
            wait_for(held.at[pl.ds(0, regions - 1), halves[0]], gather_sem.at[0])

            @pl.when(pair > 0)
            def _():
                send(held.at[:, last], first, land_sem.at[0], (r, last))

            ahead = [last - 2, last - 1, *order[3:]]
            for w in [w for w in ahead if w >= shards // 2]:
                send(held.at[:, w], first, land_sem.at[0], (r, w))
            wait_for(held.at[pl.ds(0, regions - 1), halves[1]], gather_sem.at[1])
            for w in [w for w in ahead if w < shards // 2]:
                send(held.at[:, w], first, land_sem.at[0], (r, w))
            pltpu.make_async_copy(held.at[:, 0], first, land_sem.at[0]).start()

        batches = (first, second, middle, third)
        for i in range(1, len(batches)):
            @pl.when((s >= starts[i]) & (s < starts[i + 1]))
            def _():
                spread(batches[i].at[:, :, s - starts[i]], land_sem.at[i])

        for ref, sem in ((near_of, list_sem.at[0]), (far_of, list_sem.at[1]), (weight, weight_sem)):
            wait_for(ref, sem)

        indices = [([[near_of[half, b, j] for j in range(near)] for b in range(blocks)],
                    [[(far_of[half, 0, j, b], far_of[half, 1, j, b]) for j in range(far)]
                     for b in range(blocks)])
                   for half in range(CORES)]

        def rows_of(ref, picks, m):
            return jnp.concatenate([ref[k].reshape(m, width) for k in picks], axis=1)

        pairs = range(0, blocks, 2)

        def diagonal(x, y):
            return jnp.concatenate([jnp.concatenate([x, jnp.zeros_like(y)], axis=1),
                                    jnp.concatenate([jnp.zeros_like(x), y], axis=1)], axis=0)

        def padded(x):
            short = -x.shape[0] % 16
            if not short:
                return x
            return jnp.concatenate([x, jnp.zeros((short, x.shape[1]), x.dtype)], axis=0)

        def push(half, kind, slot):
            for i, b in enumerate(pairs):
                if kind == 0 or kind == 2:
                    at = 0 if kind == 0 else near
                    w = [weight[half, c, at:at + 2].reshape(2 * width, width) for c in (b, b + 1)]
                    w = jnp.concatenate(w, axis=1)
                else:
                    at = near - 1 if kind == 1 else near + far
                    w = diagonal(weight[half, b, at], weight[half, b + 1, at])
                pltpu.matmul_push_rhs(w, slot, i)

        def side(ref, half, place, at, m):
            near_at, far_at = indices[half]
            xs = []
            for i, b in enumerate(pairs):
                if at == 1:
                    x = diagonal(*[ref[place, near_at[c][2]].reshape(m, width) for c in (b, b + 1)])
                else:
                    picks = [[(place, k) for k in near_at[c][:2]] if at == 0 else far_at[c]
                             for c in (b, b + 1)]
                    x = jnp.concatenate([rows_of(ref, p, m) for p in picks], axis=0)
                xs.append(padded(x))
            return xs

        def add(accs, xs, slot):
            for i in range(len(xs)):
                pltpu.matmul_acc_lhs(accs[i], xs[i], slot)

        def pops(accs, m):
            return [pltpu.matmul_pop(accs[i])[:2 * m] for i in range(len(pairs))]

        def scoped(f, m):
            high = 2 * m + -2 * m % 16
            pl.run_scoped(f, *[pltpu.ACC(i % len(pairs))((high, 2 * width), jnp.float32)
                               for i in range(2 * len(pairs))])

        def own_of(ref, place, m):
            both = []
            for b in pairs:
                x = [ref[place, c].reshape(m, width).astype(jnp.float32) for c in (b, b + 1)]
                x = jnp.concatenate(x, axis=0)
                both.append(jnp.concatenate([x, x], axis=1))
            return both

        def close_up(accs, half, left, m, slot, start, count):
            shape = left[0].shape
            keep = (lax.broadcasted_iota(jnp.int32, shape, 0) < m) == (
                lax.broadcasted_iota(jnp.int32, shape, 1) < width)
            means = pops(accs, m)
            rest = [padded(jnp.where(keep, x - y, 0.0).astype(jnp.bfloat16))
                    for x, y in zip(left, means)]
            add(accs[len(pairs):], rest, slot)
            for b, white in zip(pairs, pops(accs[len(pairs):], m)):
                white = white.astype(jnp.bfloat16)
                stage[half, pl.ds(start, count), b] = white[:m, :width].reshape(count, rows, width)
                stage[half, pl.ds(start, count), b + 1] = white[m:, width:].reshape(
                    count, rows, width)
            here = r - 1 + half
            for k in range(start, start + count):
                if half == 0:
                    send(stage.at[half, k], out.at[s], back_sem, (here, k))
                else:
                    @pl.when(s != k)
                    def _():
                        send(stage.at[half, k], out.at[s], back_sem, (here, k))

                    @pl.when(s == k)
                    def _():
                        pltpu.make_async_copy(stage.at[half, k], out.at[s], back_sem).start()

        def whiten(ref, sem, start, count):
            m = count * rows
            push(0, 0, 0)
            push(0, 1, 1)
            wait_for(ref, sem)

            def run(*accs):
                for half in range(CORES):
                    here = r - 1 + half
                    if half:
                        push(half, 1, 1)
                    add(accs, side(ref, half, here, 0, m), 0)
                    push(half, 2, 0)
                    add(accs, side(ref, half, here, 1, m), 1)
                    push(half, 3, 1)
                    add(accs, side(ref, half, here, 2, m), 0)
                    if half == 0:
                        push(1, 0, 0)
                    close_up(accs, half, own_of(ref, here, m), m, 1, start, count)

            scoped(run, m)

        @pl.when(farthest)
        def _():
            push(0, 0, 0)
            push(0, 1, 1)
            wait_for(early, relay_sem)
            first[close] = early[...]

            def run(*accs):
                left = []
                for half in range(CORES):
                    if half:
                        push(half, 0, 0)
                        push(half, 1, 1)
                    add(accs, side(early, half, half, 0, rows), 0)
                    add(accs, side(early, half, half, 1, rows), 1)
                    left.append([x - y for x, y in zip(own_of(early, half, rows), pops(accs, rows))])
                push(0, 2, 0)
                push(0, 3, 1)
                wait_for(first.at[remote], land_sem.at[0])
                add(accs, side(first, 0, 0, 2, rows), 0)
                push(1, 2, 0)
                close_up(accs, 0, left[0], rows, 1, 0, 1)
                push(1, 3, 1)
                add(accs, side(first, 1, 1, 2, rows), 0)
                close_up(accs, 1, left[1], rows, 1, 0, 1)

            scoped(run, rows)

        @pl.when(jnp.logical_not(farthest))
        def _():
            whiten(first, land_sem.at[0], 0, 1)

        for i in range(1, len(batches)):
            whiten(batches[i], land_sem.at[i], starts[i], starts[i + 1] - starts[i])

        for k in range(1, chips):
            wait_for(held.at[r], send_sem)
        wait_for(held.at[:, pl.ds(0, shards - 2)], send_sem)

        @pl.when((s > 0) | (pair > 0))
        def _():
            wait_for(held.at[:, 0], send_sem)

        @pl.when(fed)
        def _():
            wait_for(relay.at[0], send_sem)

        @pl.when(relays)
        def _():
            wait_for(relay, send_sem)

        wait_for(stage.at[0], send_sem)
        wait_for(stage.at[1, pl.ds(0, shards - 1)], send_sem)

    wait_for(out, back_sem)


def body(fields, near_coef, far_coef, inv_factor, near_block, far_region, far_block):
    shards, regions = lax.axis_size("shard"), lax.axis_size("region")
    rows, columns = fields.shape
    blocks, width = near_coef.shape[0], near_coef.shape[3]
    tiles = columns // width
    tiled = jnp.transpose(fields.reshape(rows, tiles, width), (1, 0, 2))
    tiled = tiled.reshape(shards, blocks, rows, width)
    hbm = pl.BlockSpec(memory_space=pl.ANY)
    half = jnp.bfloat16
    white = pl.pallas_call(
        functools.partial(kernel, regions, shards),
        out_shape=pltpu.VMEM(tiled.shape, half),
        in_specs=[hbm] * 7,
        out_specs=pl.BlockSpec(memory_space=pltpu.VMEM),
        scratch_shapes=[
            pltpu.VMEM((regions, shards, blocks, rows, width), half),
            pltpu.VMEM((regions, blocks, rows, width), half),
            pltpu.VMEM((CORES, blocks, rows, width), half),
            pltpu.VMEM((regions, blocks, rows, width), half),
            pltpu.VMEM((regions, blocks, 1, rows, width), half),
            pltpu.VMEM((regions, blocks, shards // 2 - 2, rows, width), half),
            pltpu.VMEM((regions, blocks, shards - shards // 2, rows, width), half),
            pltpu.VMEM((CORES, blocks, near_coef.shape[1] + far_coef.shape[1] + 1, width, width), half),
            pltpu.VMEM((CORES, shards, blocks, rows, width), half),
            pltpu.SMEM((CORES, *near_block.shape), jnp.int32),
            pltpu.SMEM((CORES, 2, *far_region.T.shape), jnp.int32),
            pltpu.SemaphoreType.REGULAR,
            pltpu.SemaphoreType.DMA((2,)),
            pltpu.SemaphoreType.DMA,
            pltpu.SemaphoreType.DMA,
            pltpu.SemaphoreType.DMA((2,)),
            pltpu.SemaphoreType.DMA((4,)),
            pltpu.SemaphoreType.DMA,
            pltpu.SemaphoreType.DMA,
        ],
        compiler_params=pltpu.CompilerParams(collective_id=0, has_side_effects=True),
    )(tiled, near_coef, far_coef, inv_factor, near_block, far_region.T, far_block.T)
    white = white.reshape(tiles, rows, width)
    return jnp.transpose(white, (1, 0, 2)).reshape(rows, columns)


def solution(mesh):
    return jax.shard_map(
        body,
        mesh=mesh,
        in_specs=(
            P("shard", "region"),
            P(("region", "shard"), None, None, None),
            P(("region", "shard"), None, None, None),
            P(("region", "shard"), None, None),
            P(("region", "shard"), None),
            P(("region", "shard"), None),
            P(("region", "shard"), None),
        ),
        out_specs=P("shard", "region"),
        check_vma=False,
    )
```
